512 devices in a mesh: ctx: 16 (over z, core), tis: 8 (over y), rep: 4 (over x).
Axes of the slice: x: 4, y: 8, z: 8, core: 2. Of those that a mesh axis runs over, the one named last changes fastest.
Arguments:
- donor_feat: bfloat16 [4, 256, 256], P('rep', 'ctx'), may hold values from -6 to 6
- acceptor_feat: bfloat16 [4, 256, 256], P('rep', 'ctx'), may hold values from -6 to 6
- donor_pos: int32 [4, 256], P('rep', 'ctx'), may hold values from 0 to 65535
- acceptor_pos: int32 [4, 256], P('rep'), may hold values from 0 to 65535
- pair_mask: int32 [4, 256, 80], P('rep', 'ctx'), may hold values from 0 to 1
- targets: int32 [4, 256, 32], P('rep', 'ctx', 'tis'), may hold values from 0 to 80, as said below
- dist_table: bfloat16 [128, 256], replicated, may hold values from -3 to 3
- hidden_weights: bfloat16 [32, 256, 512], P('tis'), may hold values from -0.375 to 0.375
- output_weights: bfloat16 [32, 512], P('tis')
Outputs:
- donor_loss: float32 [4, 256, 32], P('rep', 'ctx', 'tis')
- grad_hidden: float32 [32, 256, 512], P('tis', ('ctx', 'rep'))
- grad_acceptor: float32 [4, 256, 256], P('rep', 'ctx')
The draws below stay inside these ranges and needn't reach their ends.
Inputs may be any that keep to these rules, and one draw needn't show every extreme that they name: `targets`: each target is a valid slot of its donor, or 80 for no splice.
All inputs are finite; a program needn't handle non-finite values.
Results may differ from the reference program's by a relative error of at most 0.002.
The reference program's roundings to bfloat16 on the way (of `pair`, `act` and `grad_hid`) count: a program that leaves them out, or rounds other values in their place, can miss the bound.
Values may be sent and summed in bfloat16 or wider, within the bound.
A program may use at most 64 MiB of HBM per device.

```python
import math
import jax
import jax.numpy as jnp
from jax import lax

F = 256
H = 512
DON_BLK = 16
ACC_BLK = 16
BLOCK_BP = 65536
SPAN_BLOCKS = 4
BIN_BP = 2048
BINS = 128
SLOTS = 80
TISSUES = 32
SEQS = 4
DONORS = 256
ACCEPTORS = 256


def layout_draw(key):
    key_don = jax.random.fold_in(key, 11)
    key_acc = jax.random.fold_in(key, 12)
    key_mask = jax.random.fold_in(key, 13)
    key_goal = jax.random.fold_in(key, 14)
    nblocks = DONORS // DON_BLK
    reach = SPAN_BLOCKS + 1
    dpos = jax.random.randint(key_don, (SEQS, DONORS), 0, BLOCK_BP).astype(jnp.int32)
    dpos = dpos.at[0, 0].set(0).at[0, 1].set(BLOCK_BP - 1)
    apos = jax.random.randint(key_acc, (SEQS, ACCEPTORS), 0, BLOCK_BP).astype(jnp.int32)
    apos = apos.at[0, 0].set(0).at[0, 1].set(BLOCK_BP - 1)
    mask = (jax.random.randint(key_mask, (SEQS, DONORS, SLOTS), 0, 5) > 0).astype(jnp.int32)
    blocked = apos.reshape(SEQS, nblocks, ACC_BLK)
    padded = jnp.concatenate([blocked, jnp.zeros((SEQS, SPAN_BLOCKS, ACC_BLK), jnp.int32)], axis=1)
    pos_win = jnp.stack([padded[:, offset:offset + nblocks] for offset in range(reach)], axis=2).reshape(SEQS, nblocks, SLOTS)
    slot_block = jnp.arange(SLOTS, dtype=jnp.int32) // ACC_BLK
    inchain = jnp.arange(nblocks, dtype=jnp.int32)[:, None] + slot_block[None, :] < nblocks
    dist = slot_block * BLOCK_BP + pos_win[:, :, None, :] - dpos.reshape(SEQS, nblocks, DON_BLK)[..., None]
    valid = (mask.reshape(SEQS, nblocks, DON_BLK, SLOTS) > 0) & (dist > 0) & (dist <= SPAN_BLOCKS * BLOCK_BP) & inchain[None, :, None, :]
    valid = valid.reshape(SEQS, DONORS, 1, SLOTS)
    allowed = jnp.concatenate([jnp.broadcast_to(valid, (SEQS, DONORS, TISSUES, SLOTS)), jnp.ones((SEQS, DONORS, TISSUES, 1), bool)], axis=-1)
    scores = jax.random.randint(key_goal, (SEQS, DONORS, TISSUES, SLOTS + 1), 0, 2 ** 20).astype(jnp.int32)
    scores = scores * (SLOTS + 1) + jnp.arange(SLOTS + 1, dtype=jnp.int32)
    scores = jnp.where(allowed, scores, -1)
    goal = lax.top_k(scores, 1)[1][..., 0].astype(jnp.int32)
    return (dpos, apos, mask, goal)


def draw_donor_pos(key, part):
    return layout_draw(key)[0]


def draw_acceptor_pos(key, part):
    return layout_draw(key)[1]


def draw_pair_mask(key, part):
    return layout_draw(key)[2]


def draw_targets(key, part):
    return layout_draw(key)[3]


def draw_output_weights(key, part):
    values = jax.random.normal(jax.random.fold_in(key, 23), (TISSUES, H), jnp.float32)
    return (values * 2.0 / math.sqrt(H)).astype(jnp.bfloat16)


def level_of(key, dims, shards, smallest, high):
    level = 1.0
    for position, parts in shards:
        heights = jax.random.uniform(jax.random.fold_in(jax.random.fold_in(key, 6), position), (parts,), jnp.float32, smallest / len(shards), high / len(shards))
        level = level * jnp.repeat(jnp.exp(heights), dims[position] // parts).reshape((-1,) + (1,) * (len(dims) - 1 - position))
    return level


def noise(key, extent, spread, limit, cuts=(), held_as=jnp.bfloat16):
    result = spread * jax.random.normal(key, extent, jnp.float32)
    if cuts:
        result = result * level_of(key, extent, cuts, -0.22, 0.18)
    return jnp.clip(result, -limit, limit).astype(held_as)


def setup_inputs(seed: int = 0) -> dict:
    key_list = jax.random.split(jax.random.key(seed), 10)
    return {
        "donor_feat": noise(key_list[0], (SEQS, DONORS, F), 1.0, 6.0, ((0, 4), (1, 16))),
        "acceptor_feat": noise(key_list[1], (SEQS, ACCEPTORS, F), 1.0, 6.0, ((0, 4), (1, 16))),
        "donor_pos": draw_donor_pos(jax.random.fold_in(key_list[9], 71), 0),
        "acceptor_pos": draw_acceptor_pos(jax.random.fold_in(key_list[9], 71), 0),
        "pair_mask": draw_pair_mask(jax.random.fold_in(key_list[9], 71), 0),
        "targets": draw_targets(jax.random.fold_in(key_list[9], 71), 0),
        "dist_table": noise(key_list[6], (BINS, F), 0.5, 3.0),
        "hidden_weights": noise(key_list[7], (TISSUES, F, H), F ** -0.5, 0.375, ((0, 8),)),
        "output_weights": draw_output_weights(jax.random.fold_in(key_list[9], 71), 0),
    }


def silu_grad(values):
    sig = jax.nn.sigmoid(values)
    return sig * (1.0 + values * (1.0 - sig))

def reference(donor_feat, acceptor_feat, donor_pos, acceptor_pos, pair_mask, targets, dist_table, hidden_weights, output_weights):
    nblocks = DONORS // DON_BLK
    reach = SPAN_BLOCKS + 1

    def windows(stacked):
        padding = jnp.zeros((stacked.shape[0], SPAN_BLOCKS) + stacked.shape[2:], stacked.dtype)
        padded = jnp.concatenate([stacked, padding], axis=1)
        return jnp.stack([padded[:, offset:offset + nblocks] for offset in range(reach)], axis=2)
    acc_win = windows(acceptor_feat.reshape(SEQS, nblocks, ACC_BLK, F)).reshape(SEQS, nblocks, SLOTS, F)
    pos_win = windows(acceptor_pos.reshape(SEQS, nblocks, ACC_BLK)).reshape(SEQS, nblocks, SLOTS)
    slot_block = jnp.arange(SLOTS, dtype=jnp.int32) // ACC_BLK
    block_ids = jnp.arange(nblocks, dtype=jnp.int32)
    inchain = block_ids[:, None] + slot_block[None, :] < nblocks
    dpos = donor_pos.reshape(SEQS, nblocks, DON_BLK)
    dist = slot_block * BLOCK_BP + pos_win[:, :, None, :] - dpos[..., None]
    valid = (pair_mask.reshape(SEQS, nblocks, DON_BLK, SLOTS) > 0) & (dist > 0) & (dist <= SPAN_BLOCKS * BLOCK_BP) & inchain[None, :, None, :]
    bins = jnp.clip((dist - 1) // BIN_BP, 0, BINS - 1)
    table = dist_table.astype(jnp.float32)[bins]
    pre = donor_feat.astype(jnp.float32).reshape(SEQS, nblocks, DON_BLK, 1, F) + acc_win.astype(jnp.float32)[:, :, None] + table
    pair = jax.nn.silu(pre).astype(jnp.bfloat16)
    flat = pair.reshape(-1, F)
    goals = jnp.moveaxis(targets.reshape(SEQS, nblocks, DON_BLK, TISSUES), -1, 0)

    def tissue_step(grad_pair, inputs):
        w_in, w_out, goal = inputs
        hid = jnp.dot(flat, w_in, preferred_element_type=jnp.float32)
        act = jax.nn.silu(hid).astype(jnp.bfloat16)
        logits = jnp.dot(act, w_out, preferred_element_type=jnp.float32).reshape(SEQS, nblocks, DON_BLK, SLOTS)
        masked = jnp.where(valid, logits, -jnp.inf)
        top = jnp.maximum(lax.optimization_barrier(jnp.max(masked, axis=-1)), 0.0)
        expo = jnp.exp(masked - top[..., None])
        total = lax.optimization_barrier(jnp.sum(expo, axis=-1)) + jnp.exp(-top)
        picked = jnp.take_along_axis(logits, jnp.minimum(goal, SLOTS - 1)[..., None], axis=-1)[..., 0]
        picked = jnp.where(goal == SLOTS, 0.0, picked)
        loss = top + jnp.log(total) - picked
        onehot = (goal[..., None] == jnp.arange(SLOTS, dtype=jnp.int32)).astype(jnp.float32)
        grad_logits = expo / total[..., None] - onehot
        grad_act = grad_logits.reshape(-1)[:, None] * w_out.astype(jnp.float32)[None, :]
        grad_hid = (grad_act * silu_grad(hid)).astype(jnp.bfloat16)
        grad_w = jnp.dot(flat.T, grad_hid, preferred_element_type=jnp.float32)
        grad_pair = grad_pair + jnp.dot(grad_hid, w_in.T, preferred_element_type=jnp.float32)
        return (grad_pair, (loss, grad_w))
    start = jnp.zeros((flat.shape[0], F), jnp.float32)
    grad_pair, (losses, grad_hidden) = lax.scan(tissue_step, start, (hidden_weights, output_weights, goals))
    grad_pre = grad_pair.reshape(SEQS, nblocks, DON_BLK, SLOTS, F) * silu_grad(pre)
    contrib = lax.optimization_barrier(jnp.sum(grad_pre, axis=2)).reshape(SEQS, nblocks, reach, ACC_BLK, F)
    grad_acc = contrib[:, :, 0]
    for offset in range(1, reach):
        moved = jnp.concatenate([jnp.zeros((SEQS, offset, ACC_BLK, F), jnp.float32), contrib[:, :nblocks - offset, offset]], axis=1)
        grad_acc = grad_acc + moved
    donor_loss = jnp.moveaxis(losses, 0, -1).reshape(SEQS, DONORS, TISSUES)
    return (donor_loss, grad_hidden, grad_acc.reshape(SEQS, ACCEPTORS, F))
```

```python
import functools

import jax
import jax.numpy as jnp
from jax import lax
from jax.experimental import pallas as pl
from jax.experimental.pallas import tpu as pltpu
from jax.sharding import PartitionSpec as P

MESH = pl.DeviceIdType.MESH
F32 = jnp.float32
BF16 = jnp.bfloat16
BLOCK_BP = 65536
SPAN = 4
REACH = SPAN + 1
BIN_BP = 2048
BINS = 128
BLK = 16
ROWS = BLK * BLK
SLOTS = REACH * BLK
WIDTH = 256
HIDDEN = 512
LANES = 128


def kernel(
    sizes,
    don_ref,
    acc_ref,
    dpos_ref,
    apos_ref,
    mask_ref,
    goal_ref,
    table_ref,
    w_ref,
    wo_ref,
    loss_ref,
    gw_ref,
    gacc_ref,
    window,
    mpad,
    perm,
    half_pair,
    pair_t,
    slope_pre,
    valid,
    slope,
    logit,
    grad_logit,
    grad_hid,
    out_cols,
    out_rows,
    goals,
    losses,
    part,
    from_core,
    by_rep,
    from_rep,
    by_z,
    from_z,
    contrib,
    from_ctx,
    by_tis,
    halo_send,
    halo_recv,
    core_send,
    core_recv,
    rep_send,
    rep_recv,
    z_send,
    z_recv,
    ctx_send,
    ctx_recv,
    tis_send,
    tis_recv,
):
    n_ctx, n_tis, n_rep, tissues = sizes
    n_z = n_ctx // 2
    ctx = lax.axis_index("ctx")
    tis = lax.axis_index("tis")
    rep = lax.axis_index("rep")
    core = lax.rem(ctx, 2)
    z = lax.div(ctx, 2)

    def at_ctx(offset):
        return {"ctx": lax.rem(ctx + (offset % n_ctx), n_ctx)}

    def at_tis(offset):
        return {"tis": lax.rem(tis + (offset % n_tis), n_tis)}

    def at_rep(offset):
        return {"rep": lax.rem(rep + (offset % n_rep), n_rep)}

    other_core = {"ctx": ctx + 1 - 2 * core}

    def remote(src, dst, send, recv, device):
        return pltpu.make_async_remote_copy(
            src_ref=src,
            dst_ref=dst,
            send_sem=send,
            recv_sem=recv,
            device_id=device,
            device_id_type=MESH,
        )

    def halo(k):
        return remote(
            acc_ref.at[0], window.at[k], halo_send.at[k - 1], halo_recv.at[k - 1], at_ctx(-k)
        )

    def to_core(t):
        return remote(
            part.at[t, 1 - core], from_core.at[t], core_send.at[t], core_recv.at[t], other_core
        )

    def to_rep(t, j):
        return remote(
            by_rep.at[t, lax.rem(rep + j, n_rep)],
            from_rep.at[t, j - 1],
            rep_send.at[t, j - 1],
            rep_recv.at[t, j - 1],
            at_rep(j),
        )

    def to_z(t, j):
        return remote(
            by_z.at[t, lax.rem(z + j, n_z)],
            from_z.at[t, j - 1],
            z_send.at[t, j - 1],
            z_recv.at[t, j - 1],
            at_ctx(2 * j),
        )

    def to_ctx(k):
        return remote(
            contrib.at[k], from_ctx.at[k - 1], ctx_send.at[k - 1], ctx_recv.at[k - 1], at_ctx(k)
        )

    def to_tis(j):
        return remote(
            by_tis.at[tis], by_tis.at[tis], tis_send.at[j - 1], tis_recv.at[j - 1], at_tis(j)
        )

    def from_tis(j):
        came = lax.rem(tis + (n_tis - j), n_tis)
        return remote(
            by_tis.at[tis], by_tis.at[came], tis_send.at[j - 1], tis_recv.at[j - 1], at_tis(j)
        )

    barrier = pltpu.get_barrier_semaphore()
    near = set(k % n_ctx for k in range(-SPAN, SPAN + 1)) | set(range(0, n_ctx, 2))
    peers = [at_ctx(k) for k in sorted(near) if k]
    peers += [at_tis(j) for j in range(1, n_tis)] + [at_rep(j) for j in range(1, n_rep)]
    for peer in peers:
        pl.semaphore_signal(barrier, inc=1, device_id=peer, device_id_type=MESH)
    pl.semaphore_wait(barrier, len(peers))

    for k in range(1, REACH):
        halo(k).start()

    window[0] = acc_ref[0]
    mpad[...] = jnp.zeros_like(mpad)
    mpad[:, 0:SLOTS] = mask_ref[0].astype(F32)
    row = lax.broadcasted_iota(jnp.int32, (WIDTH, WIDTH), 0)
    col = lax.broadcasted_iota(jnp.int32, (WIDTH, WIDTH), 1)
    per_core = WIDTH // 2
    per_rep = per_core // n_rep
    deep = per_rep // n_z
    want = (
        (((row // deep) % n_z) * 2 + row // per_core) * (WIDTH // n_ctx)
        + ((row // per_rep) % n_rep) * deep
        + row % deep
    )
    perm[...] = jnp.where(col == want, 2.0, 0.0).astype(BF16)
    for t in range(tissues):
        line = wo_ref[t : t + 1, :].astype(F32)
        out_cols[t] = jnp.broadcast_to(line, (LANES, HIDDEN)).astype(BF16)
        out_rows[t] = jnp.broadcast_to(0.5 * line, (8, HIDDEN))
        goals[t] = jnp.broadcast_to(goal_ref[0, :, t : t + 1], (BLK, LANES))
    losses[...] = jnp.zeros_like(losses)
    eye = lax.broadcasted_iota(jnp.int32, (BLK, BLK), 0) == lax.broadcasted_iota(
        jnp.int32, (BLK, BLK), 1
    )
    dcol = jnp.sum(
        jnp.where(eye, jnp.broadcast_to(dpos_ref[...].astype(F32), (BLK, BLK)), 0.0),
        axis=1,
        keepdims=True,
    )
    dcol = jnp.broadcast_to(dcol, (BLK, LANES)).astype(jnp.int32)
    lane = lax.broadcasted_iota(jnp.int32, (BLK, BLK, LANES), 2)
    slot_in = lax.broadcasted_iota(jnp.int32, (BLK, BLK, LANES), 0)
    ones = jnp.ones((LANES, LANES), BF16)
    donors = don_ref[0].astype(F32)

    def before(k):
        base = (ctx + k) * BLK
        dist = jnp.stack(
            [
                k * BLOCK_BP + apos_ref[0, lax.rem(base + a, n_ctx * BLK)] - dcol
                for a in range(BLK)
            ]
        )
        bins = jnp.clip(lax.shift_right_arithmetic(dist - 1, 11), 0, BINS - 1)
        lookup = jnp.where(bins == lane, 1.0, 0.0).astype(BF16).reshape(ROWS, BINS)
        table = jnp.dot(lookup, table_ref[...], preferred_element_type=F32)
        picked = jnp.where(lane == slot_in + k * BLK, mpad[...][None], 0.0)
        allowed = jnp.dot(
            picked.astype(BF16).reshape(ROWS, LANES), ones, preferred_element_type=F32
        ).reshape(BLK, BLK, LANES)
        exists = ctx + k < n_ctx
        ok = (allowed > 0.5) & (dist > 0) & (dist <= SPAN * BLOCK_BP)
        ok = jnp.where(ok, 1.0, 0.0)
        valid[pl.ds(k * BLK, BLK)] = jnp.where(exists, ok, 0.0)
        feats = jnp.where(exists, window[k].astype(F32), 0.0)
        pre = table.reshape(BLK, BLK, WIDTH) + donors[None] + feats[:, None, :]
        h = 0.5 * pre.reshape(ROWS, WIDTH)
        u = jnp.tanh(h)
        p = h * u
        pair = 0.5 * (h + p).astype(BF16).astype(F32)
        half = pair.astype(BF16)
        half_pair[pl.ds(pl.multiple_of(k * ROWS, ROWS), ROWS)] = half
        slope_pre[k] = 0.5 * ((1.0 + u) * ((1.0 + h) - p))
        flipped = lax.dot_general(
            perm[...], half, (((1,), (1,)), ((), ())), preferred_element_type=F32
        ).astype(BF16)
        pair_t[k] = flipped.reshape(2, per_core, ROWS)

    before(0)
    for k in range(1, REACH):
        halo(k).wait()

    def more(k, carry):
        before(k)
        return carry

    lax.fori_loop(1, REACH, more, 0)

    slot_all = lax.broadcasted_iota(jnp.int32, (SLOTS, BLK, LANES), 0)
    lane_row = lax.broadcasted_iota(jnp.int32, (BLK, LANES), 1)

    def send_rep(t):
        to_core(t).wait()
        total = part[t, core] + from_core[t]
        by_rep[t] = total.reshape(n_rep, per_rep, HIDDEN)
        for j in range(1, n_rep):
            to_rep(t, j).start()

    def send_z(t):
        for j in range(1, n_rep):
            to_rep(t, j).wait()
        total = by_rep[t, rep]
        for j in range(1, n_rep):
            total = total + from_rep[t, j - 1]
        for i in range(n_z):
            by_z[t, i] = total[i * deep : (i + 1) * deep]
        for j in range(1, n_z):
            to_z(t, j).start()

    def weight_grad(t, side):
        total = None
        for k in range(REACH):
            term = jnp.dot(
                pair_t[k, side],
                grad_hid[t, k * ROWS : (k + 1) * ROWS],
                preferred_element_type=F32,
            )
            total = term if total is None else total + term
        part[t, side] = total

    def tissue(t, carry):
        def forward(k, carry):
            rows = pl.ds(pl.multiple_of(k * ROWS, ROWS), ROWS)
            h = jnp.dot(half_pair[rows], w_ref[t], preferred_element_type=F32)
            u = jnp.tanh(h)
            p = h * u
            slope[rows] = (1.0 + u) * ((1.0 + h) - p)
            logit[pl.ds(k * BLK, BLK)] = lax.dot_general(
                (h + p).astype(BF16),
                out_cols[t],
                (((1,), (1,)), ((), ())),
                preferred_element_type=F32,
            ).reshape(BLK, BLK, LANES)
            return carry

        lax.fori_loop(0, REACH, forward, 0)

        @pl.when(t >= 1)
        def _():
            send_rep(t - 1)

        raw = logit[...]
        ok = valid[...] > 0.5
        top = jnp.maximum(jnp.max(jnp.where(ok, raw, -jnp.inf), axis=0), 0.0)
        expo = jnp.where(ok, jnp.exp(raw - top[None]), 0.0)
        total = jnp.sum(expo, axis=0) + jnp.exp(-top)
        hit = goals[t][None] == slot_all
        grad_logit[...] = expo * (1.0 / total)[None] - jnp.where(hit, 1.0, 0.0)
        seen = jnp.sum(jnp.where(hit, raw, 0.0), axis=0)
        losses[...] = jnp.where(lane_row == t, top + jnp.log(total) - seen, losses[...])

        def backward(k, carry):
            rows = pl.ds(pl.multiple_of(k * ROWS, ROWS), ROWS)
            gl = grad_logit[pl.ds(k * BLK, BLK)].reshape(ROWS, LANES)
            wide = jnp.concatenate([gl] * (HIDDEN // LANES), axis=1)
            grad_hid[t, rows] = ((wide * out_rows[t, 0:1]) * slope[rows]).astype(BF16)
            return carry

        lax.fori_loop(0, REACH, backward, 0)

        @pl.when(t >= 1)
        def _():
            send_z(t - 1)

        weight_grad(t, 1 - core)
        to_core(t).start()
        weight_grad(t, core)
        return carry

    lax.fori_loop(0, tissues, tissue, 0)
    last = tissues - 1
    send_rep(last)
    loss_ref[0] = losses[:, 0:tissues]

    def after(step, carry):
        k = SPAN - step
        rows = pl.ds(pl.multiple_of(k * ROWS, ROWS), ROWS)
        total = None
        for t in range(tissues):
            term = lax.dot_general(
                grad_hid[t, rows],
                w_ref[t],
                (((1,), (1,)), ((), ())),
                preferred_element_type=F32,
            )
            total = term if total is None else total + term
        grad_pre = (total * slope_pre[k]).reshape(BLK, BLK, WIDTH)
        contrib[k] = jnp.sum(grad_pre, axis=1)
        return carry

    lax.fori_loop(0, REACH, after, 0)
    for k in range(1, REACH):
        to_ctx(k).start()
    send_z(last)
    total = contrib[0]
    for k in range(1, REACH):
        to_ctx(k).wait()
        total = total + from_ctx[k - 1]
    by_tis[tis] = total
    for j in range(1, n_tis):
        to_tis(j).start()

    def finish(t, carry):
        total = by_z[t, z]
        for j in range(1, n_z):
            to_z(t, j).wait()
            total = total + from_z[t, j - 1]
        gw_ref[t] = total
        return carry

    lax.fori_loop(0, tissues, finish, 0)
    for j in range(1, n_tis):
        to_tis(j).wait_send()
        from_tis(j).wait_recv()
    total = by_tis[0]
    for j in range(1, n_tis):
        total = total + by_tis[j]
    gacc_ref[0] = total


def solution(mesh):
    n_ctx, n_tis, n_rep = (mesh.shape[name] for name in ("ctx", "tis", "rep"))
    n_z = n_ctx // 2

    def on_device(don, acc, dpos, apos, mask, goal, table, w, wo):
        tissues = w.shape[0]
        per_core = WIDTH // 2
        per_rep = per_core // n_rep
        deep = per_rep // n_z
        vmem = pl.BlockSpec(memory_space=pltpu.VMEM)
        smem = pl.BlockSpec(memory_space=pltpu.SMEM)
        pairs = SLOTS * BLK
        scratch = [
            pltpu.VMEM((REACH, BLK, WIDTH), BF16),
            pltpu.VMEM((BLK, LANES), F32),
            pltpu.VMEM((WIDTH, WIDTH), BF16),
            pltpu.VMEM((pairs, WIDTH), BF16),
            pltpu.VMEM((REACH, 2, per_core, ROWS), BF16),
            pltpu.VMEM((REACH, ROWS, WIDTH), F32),
            pltpu.VMEM((SLOTS, BLK, LANES), F32),
            pltpu.VMEM((pairs, HIDDEN), F32),
            pltpu.VMEM((SLOTS, BLK, LANES), F32),
            pltpu.VMEM((SLOTS, BLK, LANES), F32),
            pltpu.VMEM((tissues, pairs, HIDDEN), BF16),
            pltpu.VMEM((tissues, LANES, HIDDEN), BF16),
            pltpu.VMEM((tissues, 8, HIDDEN), F32),
            pltpu.VMEM((tissues, BLK, LANES), jnp.int32),
            pltpu.VMEM((BLK, LANES), F32),
            pltpu.VMEM((tissues, 2, per_core, HIDDEN), F32),
            pltpu.VMEM((tissues, per_core, HIDDEN), F32),
            pltpu.VMEM((tissues, n_rep, per_rep, HIDDEN), F32),
            pltpu.VMEM((tissues, n_rep - 1, per_rep, HIDDEN), F32),
            pltpu.VMEM((tissues, n_z, deep, HIDDEN), F32),
            pltpu.VMEM((tissues, n_z - 1, deep, HIDDEN), F32),
            pltpu.VMEM((REACH, BLK, WIDTH), F32),
            pltpu.VMEM((SPAN, BLK, WIDTH), F32),
            pltpu.VMEM((n_tis, BLK, WIDTH), F32),
            pltpu.SemaphoreType.DMA((SPAN,)),
            pltpu.SemaphoreType.DMA((SPAN,)),
            pltpu.SemaphoreType.DMA((tissues,)),
            pltpu.SemaphoreType.DMA((tissues,)),
            pltpu.SemaphoreType.DMA((tissues, n_rep - 1)),
            pltpu.SemaphoreType.DMA((tissues, n_rep - 1)),
            pltpu.SemaphoreType.DMA((tissues, n_z - 1)),
            pltpu.SemaphoreType.DMA((tissues, n_z - 1)),
            pltpu.SemaphoreType.DMA((SPAN,)),
            pltpu.SemaphoreType.DMA((SPAN,)),
            pltpu.SemaphoreType.DMA((n_tis - 1,)),
            pltpu.SemaphoreType.DMA((n_tis - 1,)),
        ]
        return pl.pallas_call(
            functools.partial(kernel, (n_ctx, n_tis, n_rep, tissues)),
            out_shape=(
                jax.ShapeDtypeStruct((1, BLK, tissues), F32),
                jax.ShapeDtypeStruct((tissues, deep, HIDDEN), F32),
                jax.ShapeDtypeStruct((1, BLK, WIDTH), F32),
            ),
            in_specs=[vmem, vmem, vmem, smem, vmem, vmem, vmem, vmem, vmem],
            out_specs=(vmem, vmem, vmem),
            scratch_shapes=scratch,
            compiler_params=pltpu.CompilerParams(
                collective_id=0, has_side_effects=True, vmem_limit_bytes=44 << 20
            ),
        )(don, acc, dpos, apos, mask, goal, table, w, wo)

    placed = (
        P("rep", "ctx", None),
        P("rep", "ctx", None),
        P("rep", "ctx"),
        P("rep", None),
        P("rep", "ctx", None),
        P("rep", "ctx", "tis"),
        P(),
        P("tis", None, None),
        P("tis", None),
    )
    return jax.shard_map(
        on_device,
        mesh=mesh,
        in_specs=placed,
        out_specs=(P("rep", "ctx", "tis"), P("tis", ("ctx", "rep"), None), P("rep", "ctx", None)),
        check_vma=False,
    )
```

```python
import functools

import jax
import jax.numpy as jnp
from jax import lax
from jax.experimental import pallas as pl
from jax.experimental.pallas import tpu as pltpu
from jax.sharding import PartitionSpec as P

MESH = pl.DeviceIdType.MESH
F32 = jnp.float32
BF16 = jnp.bfloat16
BLOCK_BP = 65536
SPAN = 4
REACH = SPAN + 1
BIN_BP = 2048
BINS = 128
BLK = 16
ROWS = BLK * BLK
SLOTS = REACH * BLK
WIDTH = 256
HIDDEN = 512
LANES = 128
CHUNK = 640


def kernel(
    sizes,
    don_in,
    acc_in,
    dpos_in,
    apos_in,
    mask_in,
    goal_in,
    table_in,
    w_in,
    wo_in,
    loss_ref,
    gw_ref,
    gacc_ref,
    don_ref,
    dpos_ref,
    apos_ref,
    mask_ref,
    goal_ref,
    table_ref,
    w_ref,
    wo_ref,
    window,
    mpad,
    perm,
    half_pair,
    pair_t,
    slope_pre,
    valid,
    slope,
    logit,
    grad_logit,
    grad_hid,
    out_cols,
    out_rows,
    goals,
    losses,
    part,
    from_core,
    by_rep,
    from_first,
    from_second,
    by_z,
    from_z,
    contrib,
    from_ctx,
    by_tis,
    local,
    halo_send,
    halo_recv,
    core_send,
    core_recv,
    first_send,
    first_recv,
    second_send,
    second_recv,
    z_send,
    z_recv,
    ctx_send,
    ctx_recv,
    tis_send,
    tis_recv,
):
    n_ctx, n_tis, n_rep, tissues = sizes
    n_z = n_ctx // 2
    ctx = lax.axis_index("ctx")
    tis = lax.axis_index("tis")
    rep = lax.axis_index("rep")
    core = lax.rem(ctx, 2)
    z = lax.div(ctx, 2)

    def at_ctx(offset):
        return {"ctx": lax.rem(ctx + (offset % n_ctx), n_ctx)}

    def at_tis(offset):
        return {"tis": lax.rem(tis + (offset % n_tis), n_tis)}

    def at_rep(offset):
        return {"rep": lax.rem(rep + (offset % n_rep), n_rep)}

    other_core = {"ctx": ctx + 1 - 2 * core}

    def remote(src, dst, send, recv, device):
        return pltpu.make_async_remote_copy(
            src_ref=src,
            dst_ref=dst,
            send_sem=send,
            recv_sem=recv,
            device_id=device,
            device_id_type=MESH,
        )

    def halo(k):
        return remote(
            acc_in.at[0], window.at[k], halo_send.at[k - 1], halo_recv.at[k - 1], at_ctx(-k)
        )

    def to_core(t):
        return remote(
            part.at[t, 1 - core], from_core.at[t], core_send.at[t], core_recv.at[t], other_core
        )

    flip = (rep + 1 - 2 * lax.rem(rep, 2), n_rep - 1 - rep)
    far = lax.rem(rep + 2, n_rep)

    def to_first(t, half):
        return remote(
            by_rep.at[t, half, pl.ds(2, 2)],
            from_first.at[t, half],
            first_send.at[t, half],
            first_recv.at[t, half],
            {"rep": flip[half]},
        )

    def to_second(t, half):
        return remote(
            by_rep.at[t, half, 1],
            from_second.at[t, half],
            second_send.at[t, half],
            second_recv.at[t, half],
            {"rep": flip[1 - half]},
        )

    def to_z(t, j):
        return remote(
            by_z.at[t, lax.rem(z + j, n_z)],
            from_z.at[t, j - 1],
            z_send.at[t, j - 1],
            z_recv.at[t, j - 1],
            at_ctx(2 * j),
        )

    def to_ctx(k):
        return remote(
            contrib.at[k], from_ctx.at[k - 1], ctx_send.at[k - 1], ctx_recv.at[k - 1], at_ctx(k)
        )

    def to_tis(j):
        return remote(
            by_tis.at[tis], by_tis.at[tis], tis_send.at[j - 1], tis_recv.at[j - 1], at_tis(j)
        )

    def from_tis(j):
        came = lax.rem(tis + (n_tis - j), n_tis)
        return remote(
            by_tis.at[tis], by_tis.at[came], tis_send.at[j - 1], tis_recv.at[j - 1], at_tis(j)
        )

    staged = [
        pltpu.make_async_copy(src, dst, local.at[i])
        for i, (src, dst) in enumerate(
            [
                (apos_in, apos_ref),
                (dpos_in, dpos_ref),
                (don_in, don_ref),
                (acc_in.at[0], window.at[0]),
                (mask_in, mask_ref),
                (table_in, table_ref),
                (wo_in, wo_ref),
                (goal_in, goal_ref),
                (w_in, w_ref),
            ]
        )
    ]
    for copy in staged:
        copy.start()

    barrier = pltpu.get_barrier_semaphore()
    near = set(k % n_ctx for k in range(-SPAN, SPAN + 1)) | set(range(0, n_ctx, 2))
    peers = [at_ctx(k) for k in sorted(near) if k]
    peers += [at_tis(j) for j in range(1, n_tis)] + [at_rep(j) for j in range(1, n_rep)]
    for peer in peers:
        pl.semaphore_signal(barrier, inc=1, device_id=peer, device_id_type=MESH)
    pl.semaphore_wait(barrier, len(peers))

    for k in range(1, REACH):
        halo(k).start()

    for copy in staged[:-1]:
        copy.wait()
    mpad[...] = jnp.zeros_like(mpad)
    mpad[:, 0:SLOTS] = mask_ref[0].astype(F32)
    row = lax.broadcasted_iota(jnp.int32, (WIDTH, WIDTH), 0)
    col = lax.broadcasted_iota(jnp.int32, (WIDTH, WIDTH), 1)
    per_core = WIDTH // 2
    per_rep = per_core // n_rep
    deep = per_rep // n_z
    want = (
        (((row // deep) % n_z) * 2 + row // per_core) * (WIDTH // n_ctx)
        + ((row // per_rep) % n_rep) * deep
        + row % deep
    )
    perm[...] = jnp.where(col == want, 2.0, 0.0).astype(BF16)
    for t in range(tissues):
        line = wo_ref[t : t + 1, :].astype(F32)
        out_cols[t] = jnp.broadcast_to(line, (LANES, HIDDEN)).astype(BF16)
        out_rows[t] = jnp.broadcast_to(0.5 * line, (8, HIDDEN))
    eye = lax.broadcasted_iota(jnp.int32, (BLK, BLK), 0) == lax.broadcasted_iota(
        jnp.int32, (BLK, BLK), 1
    )

    def column(line):
        spread = jnp.where(eye, jnp.broadcast_to(line.astype(F32), (BLK, BLK)), 0.0)
        total = jnp.sum(spread, axis=1, keepdims=True)
        return jnp.broadcast_to(total, (BLK, LANES)).astype(jnp.int32)

    dcol = column(dpos_ref[...])
    for t in range(tissues):
        goals[t] = column(goal_ref[0, t : t + 1, :])
    lane = lax.broadcasted_iota(jnp.int32, (BLK, BLK, LANES), 2)
    slot_in = lax.broadcasted_iota(jnp.int32, (BLK, BLK, LANES), 0)
    ones = jnp.ones((LANES, LANES), BF16)
    donors = don_ref[0].astype(F32)

    def before(k):
        base = (ctx + k) * BLK
        dist = jnp.stack(
            [
                k * BLOCK_BP + apos_ref[0, lax.rem(base + a, n_ctx * BLK)] - dcol
                for a in range(BLK)
            ]
        )
        bins = jnp.clip(lax.shift_right_arithmetic(dist - 1, 11), 0, BINS - 1)
        lookup = jnp.where(bins == lane, 1.0, 0.0).astype(BF16).reshape(ROWS, BINS)
        table = jnp.dot(lookup, table_ref[...], preferred_element_type=F32)
        picked = jnp.where(lane == slot_in + k * BLK, mpad[...][None], 0.0)
        allowed = jnp.dot(
            picked.astype(BF16).reshape(ROWS, LANES), ones, preferred_element_type=F32
        ).reshape(BLK, BLK, LANES)
        exists = ctx + k < n_ctx
        ok = (allowed > 0.5) & (dist > 0) & (dist <= SPAN * BLOCK_BP)
        ok = jnp.where(ok, 1.0, 0.0)
        valid[pl.ds(k * BLK, BLK)] = jnp.where(exists, ok, 0.0)
        feats = jnp.where(exists, window[k].astype(F32), 0.0)
        pre = table.reshape(BLK, BLK, WIDTH) + donors[None] + feats[:, None, :]
        h = 0.5 * pre.reshape(ROWS, WIDTH)
        u = jnp.tanh(h)
        p = h * u
        pair = 0.5 * (h + p).astype(BF16).astype(F32)
        half = pair.astype(BF16)
        half_pair[pl.ds(pl.multiple_of(k * ROWS, ROWS), ROWS)] = half
        slope_pre[pl.ds(pl.multiple_of(k * ROWS, ROWS), ROWS)] = 0.5 * ((1.0 + u) * ((1.0 + h) - p))
        flipped = lax.dot_general(
            perm[...], half, (((1,), (1,)), ((), ())), preferred_element_type=F32
        ).astype(BF16)
        pair_t[:, pl.ds(pl.multiple_of(k * ROWS, ROWS), ROWS)] = flipped

    before(0)
    for k in range(1, REACH):
        halo(k).wait()

    def more(k, carry):
        before(k)
        return carry

    lax.fori_loop(1, REACH, more, 0)

    slot_all = lax.broadcasted_iota(jnp.int32, (SLOTS, BLK, LANES), 0)
    lane_row = lax.broadcasted_iota(jnp.int32, (BLK, LANES), 1)

    def send_first(t):
        to_core(t).wait()
        for half in range(2):
            for i, q in enumerate((rep, flip[1 - half], flip[half], far)):
                rows = pl.ds(pl.multiple_of(q * per_rep, per_rep), per_rep)
                by_rep[t, half, i] = part[t, core, half, rows] + from_core[t, half, rows]
            to_first(t, half).start()

    def send_second(t):
        for half in range(2):
            to_first(t, half).wait()
            by_rep[t, half, 1] = by_rep[t, half, 1] + from_first[t, half, 1]
            to_second(t, half).start()

    def send_z(t):
        for half in range(2):
            to_second(t, half).wait()
            total = by_rep[t, half, 0] + from_first[t, half, 0] + from_second[t, half]
            for i in range(n_z):
                by_z[t, i, :, half * WIDTH : (half + 1) * WIDTH] = total[i * deep : (i + 1) * deep]
        for j in range(1, n_z):
            to_z(t, j).start()

    def weight_grad(t):
        total = jnp.dot(pair_t[...], grad_hid[t], preferred_element_type=F32)
        total = total.reshape(2, per_core, HIDDEN)
        part[t, :, 0] = total[:, :, :WIDTH]
        part[t, :, 1] = total[:, :, WIDTH:]

    staged[-1].wait()

    def tissue(t, carry):
        def forward(k, carry):
            rows = pl.ds(pl.multiple_of(k * CHUNK, CHUNK), CHUNK)
            h = jnp.dot(half_pair[rows], w_ref[t], preferred_element_type=F32)
            u = jnp.tanh(h)
            p = h * u
            slope[rows] = (1.0 + u) * ((1.0 + h) - p)
            logit[pl.ds(k * (CHUNK // BLK), CHUNK // BLK)] = lax.dot_general(
                (h + p).astype(BF16),
                out_cols[t],
                (((1,), (1,)), ((), ())),
                preferred_element_type=F32,
            ).reshape(CHUNK // BLK, BLK, LANES)
            return carry

        lax.fori_loop(0, SLOTS * BLK // CHUNK, forward, 0)

        @pl.when(t >= 1)
        def _():
            send_first(t - 1)

        @pl.when(t >= 2)
        def _():
            send_second(t - 2)

        raw = logit[...]
        ok = valid[...] > 0.5
        top = jnp.maximum(jnp.max(jnp.where(ok, raw, -jnp.inf), axis=0), 0.0)
        expo = jnp.where(ok, jnp.exp(raw - top[None]), 0.0)
        total = jnp.sum(expo, axis=0) + jnp.exp(-top)
        hit = goals[t][None] == slot_all
        grad_logit[...] = expo * (1.0 / total)[None] - jnp.where(hit, 1.0, 0.0)
        seen = jnp.sum(jnp.where(hit, raw, 0.0), axis=0)
        losses[t] = top + jnp.log(total) - seen

        def backward(k, carry):
            rows = pl.ds(pl.multiple_of(k * ROWS, ROWS), ROWS)
            gl = grad_logit[pl.ds(k * BLK, BLK)].reshape(ROWS, LANES)
            wide = jnp.concatenate([gl] * (HIDDEN // LANES), axis=1)
            grad_hid[t, rows] = ((wide * out_rows[t, 0:1]) * slope[rows]).astype(BF16)
            return carry

        lax.fori_loop(0, REACH, backward, 0)

        weight_grad(t)
        to_core(t).start()

        @pl.when(t >= 2)
        def _():
            send_z(t - 2)

        return carry

    lax.fori_loop(0, tissues, tissue, 0)
    last = tissues - 1
    send_second(last - 1)

    def after(low, high):
        rows = slice(low * ROWS, high * ROWS)
        total = None
        for t in range(tissues):
            term = lax.dot_general(
                grad_hid[t, rows],
                w_ref[t],
                (((1,), (1,)), ((), ())),
                preferred_element_type=F32,
            )
            total = term if total is None else total + term
        grad_pre = (total * slope_pre[rows]).reshape((high - low) * BLK, BLK, WIDTH)
        contrib[low:high] = jnp.sum(grad_pre, axis=1).reshape(high - low, BLK, WIDTH)
        for k in range(max(low, 1), high):
            to_ctx(k).start()

    send_first(last)
    after(3, REACH)
    send_z(last - 1)
    send_second(last)
    after(0, 3)
    send_z(last)
    total = contrib[0]
    for k in range(1, REACH):
        to_ctx(k).wait()
        total = total + from_ctx[k - 1]
    by_tis[tis] = total
    for j in range(1, n_tis):
        to_tis(j).start()
    wide_eye = lax.broadcasted_iota(jnp.int32, (BLK, LANES), 0) == lane_row
    for t in range(tissues):
        line = jnp.sum(jnp.where(wide_eye, losses[t], 0.0), axis=0, keepdims=True)
        loss_ref[0, t : t + 1, :] = line[:, 0:BLK]

    def finish(t, carry):
        total = by_z[t, z]
        for j in range(1, n_z):
            to_z(t, j).wait()
            total = total + from_z[t, j - 1]
        gw_ref[t] = total
        return carry

    lax.fori_loop(0, tissues, finish, 0)
    for j in range(1, n_tis):
        to_tis(j).wait_send()
        from_tis(j).wait_recv()
    total = by_tis[0]
    for j in range(1, n_tis):
        total = total + by_tis[j]
    gacc_ref[0] = total


def solution(mesh):
    n_ctx, n_tis, n_rep = (mesh.shape[name] for name in ("ctx", "tis", "rep"))
    n_z = n_ctx // 2

    def on_device(don, acc, dpos, apos, mask, goal, table, w, wo):
        tissues = w.shape[0]
        per_core = WIDTH // 2
        per_rep = per_core // n_rep
        deep = per_rep // n_z
        vmem = pl.BlockSpec(memory_space=pltpu.VMEM)
        hbm = pl.BlockSpec(memory_space=pltpu.HBM)
        pairs = SLOTS * BLK
        scratch = [
            pltpu.VMEM((1, BLK, WIDTH), BF16),
            pltpu.VMEM((1, BLK), jnp.int32),
            pltpu.SMEM((1, n_ctx * BLK), jnp.int32),
            pltpu.VMEM((1, BLK, SLOTS), jnp.int32),
            pltpu.VMEM((1, tissues, BLK), jnp.int32),
            pltpu.VMEM((BINS, WIDTH), BF16),
            pltpu.VMEM((tissues, WIDTH, HIDDEN), BF16),
            pltpu.VMEM((tissues, HIDDEN), BF16),
            pltpu.VMEM((REACH, BLK, WIDTH), BF16),
            pltpu.VMEM((BLK, LANES), F32),
            pltpu.VMEM((WIDTH, WIDTH), BF16),
            pltpu.VMEM((pairs, WIDTH), BF16),
            pltpu.VMEM((WIDTH, pairs), BF16),
            pltpu.VMEM((pairs, WIDTH), F32),
            pltpu.VMEM((SLOTS, BLK, LANES), F32),
            pltpu.VMEM((pairs, HIDDEN), F32),
            pltpu.VMEM((SLOTS, BLK, LANES), F32),
            pltpu.VMEM((SLOTS, BLK, LANES), F32),
            pltpu.VMEM((tissues, pairs, HIDDEN), BF16),
            pltpu.VMEM((tissues, LANES, HIDDEN), BF16),
            pltpu.VMEM((tissues, 8, HIDDEN), F32),
            pltpu.VMEM((tissues, BLK, LANES), jnp.int32),
            pltpu.VMEM((tissues, BLK, LANES), F32),
            pltpu.VMEM((tissues, 2, 2, per_core, WIDTH), F32),
            pltpu.VMEM((tissues, 2, per_core, WIDTH), F32),
            pltpu.VMEM((tissues, 2, n_rep, per_rep, WIDTH), F32),
            pltpu.VMEM((tissues, 2, 2, per_rep, WIDTH), F32),
            pltpu.VMEM((tissues, 2, per_rep, WIDTH), F32),
            pltpu.VMEM((tissues, n_z, deep, HIDDEN), F32),
            pltpu.VMEM((tissues, n_z - 1, deep, HIDDEN), F32),
            pltpu.VMEM((REACH, BLK, WIDTH), F32),
            pltpu.VMEM((SPAN, BLK, WIDTH), F32),
            pltpu.VMEM((n_tis, BLK, WIDTH), F32),
            pltpu.SemaphoreType.DMA((9,)),
            pltpu.SemaphoreType.DMA((SPAN,)),
            pltpu.SemaphoreType.DMA((SPAN,)),
            pltpu.SemaphoreType.DMA((tissues,)),
            pltpu.SemaphoreType.DMA((tissues,)),
            pltpu.SemaphoreType.DMA((tissues, 2)),
            pltpu.SemaphoreType.DMA((tissues, 2)),
            pltpu.SemaphoreType.DMA((tissues, 2)),
            pltpu.SemaphoreType.DMA((tissues, 2)),
            pltpu.SemaphoreType.DMA((tissues, n_z - 1)),
            pltpu.SemaphoreType.DMA((tissues, n_z - 1)),
            pltpu.SemaphoreType.DMA((SPAN,)),
            pltpu.SemaphoreType.DMA((SPAN,)),
            pltpu.SemaphoreType.DMA((n_tis - 1,)),
            pltpu.SemaphoreType.DMA((n_tis - 1,)),
        ]
        loss, grad_hidden, grad_acceptor = pl.pallas_call(
            functools.partial(kernel, (n_ctx, n_tis, n_rep, tissues)),
            out_shape=(
                jax.ShapeDtypeStruct((1, tissues, BLK), F32),
                jax.ShapeDtypeStruct((tissues, deep, HIDDEN), F32),
                jax.ShapeDtypeStruct((1, BLK, WIDTH), F32),
            ),
            in_specs=[hbm] * 9,
            out_specs=(vmem, vmem, vmem),
            scratch_shapes=scratch,
            compiler_params=pltpu.CompilerParams(
                collective_id=0, has_side_effects=True, vmem_limit_bytes=60 << 20
            ),
        )(don, acc, dpos, apos, mask, jnp.swapaxes(goal, 1, 2), table, w, wo)
        return jnp.swapaxes(loss, 1, 2), grad_hidden, grad_acceptor

    placed = (
        P("rep", "ctx", None),
        P("rep", "ctx", None),
        P("rep", "ctx"),
        P("rep", None),
        P("rep", "ctx", None),
        P("rep", "ctx", "tis"),
        P(),
        P("tis", None, None),
        P("tis", None),
    )
    return jax.shard_map(
        on_device,
        mesh=mesh,
        in_specs=placed,
        out_specs=(P("rep", "ctx", "tis"), P("tis", ("ctx", "rep"), None), P("rep", "ctx", None)),
        check_vma=False,
    )
```

```python
import functools

import jax
import jax.numpy as jnp
from jax import lax
from jax.experimental import pallas as pl
from jax.experimental.pallas import tpu as pltpu
from jax.sharding import PartitionSpec as P

MESH = pl.DeviceIdType.MESH
F32 = jnp.float32
BF16 = jnp.bfloat16
BLOCK_BP = 65536
SPAN = 4
REACH = SPAN + 1
BIN_BP = 2048
BINS = 128
BLK = 16
ROWS = BLK * BLK
SLOTS = REACH * BLK
WIDTH = 256
HIDDEN = 512
LANES = 128
CHUNK = 640


def kernel(
    sizes,
    don_in,
    acc_in,
    dpos_in,
    apos_in,
    mask_in,
    goal_in,
    table_in,
    w_in,
    wo_in,
    loss_ref,
    gw_ref,
    gacc_ref,
    don_ref,
    dpos_ref,
    apos_ref,
    mask_ref,
    goal_ref,
    table_ref,
    w_ref,
    wo_ref,
    window,
    mpad,
    perm,
    half_pair,
    pair_t,
    half_pre,
    valid,
    slope,
    logit,
    grad_logit,
    grad_hid,
    out_cols,
    out_rows,
    goals,
    losses,
    part,
    from_core,
    by_rep,
    from_first,
    from_second,
    by_z,
    from_z,
    contrib,
    from_ctx,
    by_tis,
    local,
    halo_send,
    halo_recv,
    core_send,
    core_recv,
    first_send,
    first_recv,
    second_send,
    second_recv,
    z_send,
    z_recv,
    ctx_send,
    ctx_recv,
    tis_send,
    tis_recv,
):
    n_ctx, n_tis, n_rep, tissues = sizes
    n_z = n_ctx // 2
    ctx = lax.axis_index("ctx")
    tis = lax.axis_index("tis")
    rep = lax.axis_index("rep")
    core = lax.rem(ctx, 2)
    z = lax.div(ctx, 2)

    def at_ctx(offset):
        return {"ctx": lax.rem(ctx + (offset % n_ctx), n_ctx)}

    def at_tis(offset):
        return {"tis": lax.rem(tis + (offset % n_tis), n_tis)}

    def at_rep(offset):
        return {"rep": lax.rem(rep + (offset % n_rep), n_rep)}

    other_core = {"ctx": ctx + 1 - 2 * core}

    def remote(src, dst, send, recv, device):
        return pltpu.make_async_remote_copy(
            src_ref=src,
            dst_ref=dst,
            send_sem=send,
            recv_sem=recv,
            device_id=device,
            device_id_type=MESH,
        )

    def halo(k):
        return remote(
            acc_in.at[0], window.at[k], halo_send.at[k - 1], halo_recv.at[k - 1], at_ctx(-k)
        )

    def to_core(t):
        return remote(
            part.at[t, 1 - core], from_core.at[t], core_send.at[t], core_recv.at[t], other_core
        )

    flip = (rep + 1 - 2 * lax.rem(rep, 2), n_rep - 1 - rep)
    far = lax.rem(rep + 2, n_rep)

    def to_first(t, half):
        return remote(
            by_rep.at[t, half, pl.ds(2, 2)],
            from_first.at[t, half],
            first_send.at[t, half],
            first_recv.at[t, half],
            {"rep": flip[half]},
        )

    def to_second(t, half):
        return remote(
            by_rep.at[t, half, 1],
            from_second.at[t, half],
            second_send.at[t, half],
            second_recv.at[t, half],
            {"rep": flip[1 - half]},
        )

    def to_z(t, j):
        return remote(
            by_z.at[t, lax.rem(z + j, n_z)],
            from_z.at[t, j - 1],
            z_send.at[t, j - 1],
            z_recv.at[t, j - 1],
            at_ctx(2 * j),
        )

    def to_ctx(k):
        return remote(
            contrib.at[k], from_ctx.at[k - 1], ctx_send.at[k - 1], ctx_recv.at[k - 1], at_ctx(k)
        )

    def to_tis(j):
        return remote(
            by_tis.at[tis], by_tis.at[tis], tis_send.at[j - 1], tis_recv.at[j - 1], at_tis(j)
        )

    def from_tis(j):
        came = lax.rem(tis + (n_tis - j), n_tis)
        return remote(
            by_tis.at[tis], by_tis.at[came], tis_send.at[j - 1], tis_recv.at[j - 1], at_tis(j)
        )

    staged = [
        pltpu.make_async_copy(src, dst, local.at[i])
        for i, (src, dst) in enumerate(
            [
                (apos_in, apos_ref),
                (dpos_in, dpos_ref),
                (don_in, don_ref),
                (acc_in.at[0], window.at[0]),
                (mask_in, mask_ref),
                (table_in, table_ref),
                (wo_in, wo_ref),
                (goal_in, goal_ref),
                (w_in, w_ref),
            ]
        )
    ]
    for copy in staged:
        copy.start()

    barrier = pltpu.get_barrier_semaphore()
    near = set(k % n_ctx for k in range(-SPAN, SPAN + 1)) | set(range(0, n_ctx, 2))
    peers = [at_ctx(k) for k in sorted(near) if k]
    peers += [at_tis(j) for j in range(1, n_tis)] + [at_rep(j) for j in range(1, n_rep)]
    for peer in peers:
        pl.semaphore_signal(barrier, inc=1, device_id=peer, device_id_type=MESH)
    for copy in staged[:-1]:
        copy.wait()
    mpad[...] = jnp.zeros_like(mpad)
    mpad[:, 0:SLOTS] = mask_ref[0].astype(F32)
    row = lax.broadcasted_iota(jnp.int32, (WIDTH, WIDTH), 0)
    col = lax.broadcasted_iota(jnp.int32, (WIDTH, WIDTH), 1)
    per_core = WIDTH // 2
    per_rep = per_core // n_rep
    deep = per_rep // n_z
    want = (
        (((row // deep) % n_z) * 2 + row // per_core) * (WIDTH // n_ctx)
        + ((row // per_rep) % n_rep) * deep
        + row % deep
    )
    perm[...] = jnp.where(col == want, 2.0, 0.0).astype(BF16)
    for t in range(tissues):
        line = wo_ref[t : t + 1, :].astype(F32)
        out_cols[t] = jnp.broadcast_to(line, (LANES, HIDDEN)).astype(BF16)
        out_rows[t] = jnp.broadcast_to(0.5 * line, (8, HIDDEN))
    eye = lax.broadcasted_iota(jnp.int32, (BLK, BLK), 0) == lax.broadcasted_iota(
        jnp.int32, (BLK, BLK), 1
    )

    def column(line):
        spread = jnp.where(eye, jnp.broadcast_to(line.astype(F32), (BLK, BLK)), 0.0)
        total = jnp.sum(spread, axis=1, keepdims=True)
        return jnp.broadcast_to(total, (BLK, LANES)).astype(jnp.int32)

    dcol = column(dpos_ref[...])
    for t in range(tissues):
        goals[t] = column(goal_ref[0, t : t + 1, :])
    pl.semaphore_wait(barrier, len(peers))

    for k in reversed(range(1, REACH)):
        halo(k).start()

    lane = lax.broadcasted_iota(jnp.int32, (BLK, BLK, LANES), 2)
    slot_in = lax.broadcasted_iota(jnp.int32, (BLK, BLK, LANES), 0)
    ones = jnp.ones((LANES, LANES), BF16)
    donors = don_ref[0].astype(F32)

    def before(k):
        base = (ctx + k) * BLK
        dist = jnp.stack(
            [
                k * BLOCK_BP + apos_ref[0, lax.rem(base + a, n_ctx * BLK)] - dcol
                for a in range(BLK)
            ]
        )
        bins = jnp.clip(lax.shift_right_arithmetic(dist - 1, 11), 0, BINS - 1)
        lookup = jnp.where(bins == lane, 1.0, 0.0).astype(BF16).reshape(ROWS, BINS)
        table = jnp.dot(lookup, table_ref[...], preferred_element_type=F32)
        picked = jnp.where(lane == slot_in + k * BLK, mpad[...][None], 0.0)
        allowed = jnp.dot(
            picked.astype(BF16).reshape(ROWS, LANES), ones, preferred_element_type=F32
        ).reshape(BLK, BLK, LANES)
        exists = ctx + k < n_ctx
        ok = (allowed > 0.5) & (dist > 0) & (dist <= SPAN * BLOCK_BP)
        ok = jnp.where(ok, 1.0, 0.0)
        valid[pl.ds(k * BLK, BLK)] = jnp.where(exists, ok, 0.0)
        feats = jnp.where(exists, window[k].astype(F32), 0.0)
        pre = table.reshape(BLK, BLK, WIDTH) + donors[None] + feats[:, None, :]
        h = 0.5 * pre.reshape(ROWS, WIDTH)
        u = jnp.tanh(h)
        p = h * u
        pair = 0.5 * (h + p).astype(BF16).astype(F32)
        half = pair.astype(BF16)
        half_pair[pl.ds(pl.multiple_of(k * ROWS, ROWS), ROWS)] = half
        half_pre[pl.ds(pl.multiple_of(k * ROWS, ROWS), ROWS)] = h
        flipped = lax.dot_general(
            perm[...], half, (((1,), (1,)), ((), ())), preferred_element_type=F32
        ).astype(BF16)
        pair_t[:, pl.ds(pl.multiple_of(k * ROWS, ROWS), ROWS)] = flipped

    before(0)

    def more(k, carry):
        halo(k).wait()
        before(k)
        return carry

    lax.fori_loop(1, REACH, more, 0)

    slot_all = lax.broadcasted_iota(jnp.int32, (SLOTS, BLK, LANES), 0)
    lane_row = lax.broadcasted_iota(jnp.int32, (BLK, LANES), 1)

    def send_first(t):
        to_core(t).wait()
        for half in range(2):
            for i, q in enumerate((rep, flip[1 - half], flip[half], far)):
                rows = pl.ds(pl.multiple_of(q * per_rep, per_rep), per_rep)
                by_rep[t, half, i] = part[t, core, half, rows] + from_core[t, half, rows]
            to_first(t, half).start()

    def send_second(t):
        for half in range(2):
            to_first(t, half).wait()
            by_rep[t, half, 1] = by_rep[t, half, 1] + from_first[t, half, 1]
            to_second(t, half).start()

    def send_z(t):
        for half in range(2):
            to_second(t, half).wait()
            total = by_rep[t, half, 0] + from_first[t, half, 0] + from_second[t, half]
            for i in range(n_z):
                by_z[t, i, :, half * WIDTH : (half + 1) * WIDTH] = total[i * deep : (i + 1) * deep]
        for j in range(1, n_z):
            to_z(t, j).start()

    def weight_grad(t):
        total = jnp.dot(pair_t[...], grad_hid[t], preferred_element_type=F32)
        total = total.reshape(2, per_core, HIDDEN)
        part[t, :, 0] = total[:, :, :WIDTH]
        part[t, :, 1] = total[:, :, WIDTH:]

    staged[-1].wait()

    def tissue(t, carry):
        def forward(k):
            rows = slice(k * CHUNK, (k + 1) * CHUNK)
            h = jnp.dot(half_pair[rows], w_ref[t], preferred_element_type=F32)
            u = jnp.tanh(h)
            p = h * u
            slope[rows] = (1.0 + u) * ((1.0 + h) - p)
            logit[k * (CHUNK // BLK) : (k + 1) * (CHUNK // BLK)] = lax.dot_general(
                (h + p).astype(BF16),
                out_cols[t],
                (((1,), (1,)), ((), ())),
                preferred_element_type=F32,
            ).reshape(CHUNK // BLK, BLK, LANES)

        for k in range(SLOTS * BLK // CHUNK):
            forward(k)

        @pl.when(t >= 3)
        def _():
            send_second(t - 3)

        raw = logit[...]
        ok = valid[...] > 0.5
        top = jnp.maximum(jnp.max(jnp.where(ok, raw, -jnp.inf), axis=0), 0.0)
        expo = jnp.where(ok, jnp.exp(raw - top[None]), 0.0)
        total = jnp.sum(expo, axis=0) + jnp.exp(-top)
        hit = goals[t][None] == slot_all
        grad_logit[...] = expo * (1.0 / total)[None] - jnp.where(hit, 1.0, 0.0)
        seen = jnp.sum(jnp.where(hit, raw, 0.0), axis=0)
        losses[t] = top + jnp.log(total) - seen

        for k in range(REACH):
            rows = slice(k * ROWS, (k + 1) * ROWS)
            gl = grad_logit[k * BLK : (k + 1) * BLK].reshape(ROWS, LANES)
            wide = jnp.concatenate([gl] * (HIDDEN // LANES), axis=1)
            grad_hid[t, rows] = ((wide * out_rows[t, 0:1]) * slope[rows]).astype(BF16)

        weight_grad(t)
        to_core(t).start()

        @pl.when(t >= 1)
        def _():
            send_first(t - 1)

        return carry

    lax.fori_loop(0, tissues, tissue, 0)
    last = tissues - 1
    def after(low, high):
        rows = slice(low * ROWS, high * ROWS)
        total = None
        for t in range(tissues):
            term = lax.dot_general(
                grad_hid[t, rows],
                w_ref[t],
                (((1,), (1,)), ((), ())),
                preferred_element_type=F32,
            )
            total = term if total is None else total + term
        h = half_pre[rows]
        u = jnp.tanh(h)
        steep = 0.5 * ((1.0 + u) * ((1.0 + h) - h * u))
        grad_pre = (total * steep).reshape((high - low) * BLK, BLK, WIDTH)
        contrib[low:high] = jnp.sum(grad_pre, axis=1).reshape(high - low, BLK, WIDTH)
        for k in range(max(low, 1), high):
            to_ctx(k).start()

    after(3, REACH)
    send_second(last - 2)
    send_z(last - 3)
    send_first(last)
    after(0, 3)
    send_second(last - 1)
    send_z(last - 2)
    send_second(last)
    send_z(last - 1)
    total = contrib[0]
    for k in range(1, REACH):
        to_ctx(k).wait()
        total = total + from_ctx[k - 1]
    by_tis[tis] = total
    for j in range(1, n_tis):
        to_tis(j).start()
    send_z(last)
    wide_eye = lax.broadcasted_iota(jnp.int32, (BLK, LANES), 0) == lane_row
    for t in range(tissues):
        line = jnp.sum(jnp.where(wide_eye, losses[t], 0.0), axis=0, keepdims=True)
        loss_ref[0, t : t + 1, :] = line[:, 0:BLK]

    def finish(t, carry):
        total = by_z[t, z]
        for j in range(1, n_z):
            to_z(t, j).wait()
            total = total + from_z[t, j - 1]
        gw_ref[t] = total
        return carry

    lax.fori_loop(0, tissues, finish, 0)
    for j in range(1, n_tis):
        to_tis(j).wait_send()
        from_tis(j).wait_recv()
    total = by_tis[0]
    for j in range(1, n_tis):
        total = total + by_tis[j]
    gacc_ref[0] = total


def hand_over(*refs):
    sems = refs[6]
    copies = [
        pltpu.make_async_copy(refs[i], refs[3 + i], sems.at[i]) for i in range(3)
    ]
    for copy in copies:
        copy.start()
    for copy in copies:
        copy.wait()


def solution(mesh):
    n_ctx, n_tis, n_rep = (mesh.shape[name] for name in ("ctx", "tis", "rep"))
    n_z = n_ctx // 2

    def on_device(don, acc, dpos, apos, mask, goal, table, w, wo):
        tissues = w.shape[0]
        per_core = WIDTH // 2
        per_rep = per_core // n_rep
        deep = per_rep // n_z
        vmem = pl.BlockSpec(memory_space=pltpu.VMEM)
        hbm = pl.BlockSpec(memory_space=pltpu.HBM)
        pairs = SLOTS * BLK
        scratch = [
            pltpu.VMEM((1, BLK, WIDTH), BF16),
            pltpu.VMEM((1, BLK), jnp.int32),
            pltpu.SMEM((1, n_ctx * BLK), jnp.int32),
            pltpu.VMEM((1, BLK, SLOTS), jnp.int32),
            pltpu.VMEM((1, tissues, BLK), jnp.int32),
            pltpu.VMEM((BINS, WIDTH), BF16),
            pltpu.VMEM((tissues, WIDTH, HIDDEN), BF16),
            pltpu.VMEM((tissues, HIDDEN), BF16),
            pltpu.VMEM((REACH, BLK, WIDTH), BF16),
            pltpu.VMEM((BLK, LANES), F32),
            pltpu.VMEM((WIDTH, WIDTH), BF16),
            pltpu.VMEM((pairs, WIDTH), BF16),
            pltpu.VMEM((WIDTH, pairs), BF16),
            pltpu.VMEM((pairs, WIDTH), F32),
            pltpu.VMEM((SLOTS, BLK, LANES), F32),
            pltpu.VMEM((pairs, HIDDEN), F32),
            pltpu.VMEM((SLOTS, BLK, LANES), F32),
            pltpu.VMEM((SLOTS, BLK, LANES), F32),
            pltpu.VMEM((tissues, pairs, HIDDEN), BF16),
            pltpu.VMEM((tissues, LANES, HIDDEN), BF16),
            pltpu.VMEM((tissues, 8, HIDDEN), F32),
            pltpu.VMEM((tissues, BLK, LANES), jnp.int32),
            pltpu.VMEM((tissues, BLK, LANES), F32),
            pltpu.VMEM((tissues, 2, 2, per_core, WIDTH), F32),
            pltpu.VMEM((tissues, 2, per_core, WIDTH), F32),
            pltpu.VMEM((tissues, 2, n_rep, per_rep, WIDTH), F32),
            pltpu.VMEM((tissues, 2, 2, per_rep, WIDTH), F32),
            pltpu.VMEM((tissues, 2, per_rep, WIDTH), F32),
            pltpu.VMEM((tissues, n_z, deep, HIDDEN), F32),
            pltpu.VMEM((tissues, n_z - 1, deep, HIDDEN), F32),
            pltpu.VMEM((REACH, BLK, WIDTH), F32),
            pltpu.VMEM((SPAN, BLK, WIDTH), F32),
            pltpu.VMEM((n_tis, BLK, WIDTH), F32),
            pltpu.SemaphoreType.DMA((9,)),
            pltpu.SemaphoreType.DMA((SPAN,)),
            pltpu.SemaphoreType.DMA((SPAN,)),
            pltpu.SemaphoreType.DMA((tissues,)),
            pltpu.SemaphoreType.DMA((tissues,)),
            pltpu.SemaphoreType.DMA((tissues, 2)),
            pltpu.SemaphoreType.DMA((tissues, 2)),
            pltpu.SemaphoreType.DMA((tissues, 2)),
            pltpu.SemaphoreType.DMA((tissues, 2)),
            pltpu.SemaphoreType.DMA((tissues, n_z - 1)),
            pltpu.SemaphoreType.DMA((tissues, n_z - 1)),
            pltpu.SemaphoreType.DMA((SPAN,)),
            pltpu.SemaphoreType.DMA((SPAN,)),
            pltpu.SemaphoreType.DMA((n_tis - 1,)),
            pltpu.SemaphoreType.DMA((n_tis - 1,)),
        ]
        results = pl.pallas_call(
            functools.partial(kernel, (n_ctx, n_tis, n_rep, tissues)),
            out_shape=(
                jax.ShapeDtypeStruct((1, tissues, BLK), F32),
                jax.ShapeDtypeStruct((tissues, deep, HIDDEN), F32),
                jax.ShapeDtypeStruct((1, BLK, WIDTH), F32),
            ),
            in_specs=[hbm] * 9,
            out_specs=(vmem, vmem, vmem),
            scratch_shapes=scratch,
            compiler_params=pltpu.CompilerParams(
                collective_id=0, has_side_effects=True, vmem_limit_bytes=60 << 20
            ),
        )(don, acc, dpos, apos, mask, jnp.swapaxes(goal, 1, 2), table, w, wo)
        loss, grad_hidden, grad_acceptor = pl.pallas_call(
            hand_over,
            out_shape=tuple(jax.ShapeDtypeStruct(r.shape, r.dtype) for r in results),
            in_specs=[vmem] * 3,
            out_specs=(hbm,) * 3,
            scratch_shapes=[pltpu.SemaphoreType.DMA((3,))],
        )(*results)
        return jnp.swapaxes(loss, 1, 2), grad_hidden, grad_acceptor

    placed = (
        P("rep", "ctx", None),
        P("rep", "ctx", None),
        P("rep", "ctx"),
        P("rep", None),
        P("rep", "ctx", None),
        P("rep", "ctx", "tis"),
        P(),
        P("tis", None, None),
        P("tis", None),
    )
    return jax.shard_map(
        on_device,
        mesh=mesh,
        in_specs=placed,
        out_specs=(P("rep", "ctx", "tis"), P("tis", ("ctx", "rep"), None), P("rep", "ctx", None)),
        check_vma=False,
    )
```

```python
import functools

import jax
import jax.numpy as jnp
from jax import lax
from jax.experimental import pallas as pl
from jax.experimental.pallas import tpu as pltpu
from jax.sharding import PartitionSpec as P

MESH = pl.DeviceIdType.MESH
F32 = jnp.float32
BF16 = jnp.bfloat16
BLOCK_BP = 65536
SPAN = 4
REACH = SPAN + 1
BIN_BP = 2048
BINS = 128
BLK = 16
ROWS = BLK * BLK
SLOTS = REACH * BLK
WIDTH = 256
HIDDEN = 512
LANES = 128


def kernel(
    sizes,
    don_in,
    acc_in,
    dpos_in,
    apos_in,
    mask_in,
    goal_in,
    table_in,
    w_in,
    wo_in,
    loss_ref,
    gw_ref,
    gacc_ref,
    don_ref,
    dpos_ref,
    apos_ref,
    mask_ref,
    goal_ref,
    table_ref,
    w_ref,
    wo_ref,
    window,
    mpad,
    perm,
    half_pair,
    pair_t,
    half_pre,
    valid,
    slope,
    logit,
    grad_logit,
    grad_hid,
    out_cols,
    out_rows,
    goals,
    losses,
    part,
    from_core,
    by_rep,
    from_first,
    from_second,
    last_own,
    last_rep,
    from_rep,
    by_z,
    from_z,
    contrib,
    from_ctx,
    by_tis,
    local,
    halo_send,
    halo_recv,
    core_send,
    core_recv,
    first_send,
    first_recv,
    second_send,
    second_recv,
    rep_send,
    rep_recv,
    z_send,
    z_recv,
    ctx_send,
    ctx_recv,
    tis_send,
    tis_recv,
):
    n_ctx, n_tis, n_rep, tissues = sizes
    n_z = n_ctx // 2
    ctx = lax.axis_index("ctx")
    tis = lax.axis_index("tis")
    rep = lax.axis_index("rep")
    core = lax.rem(ctx, 2)
    z = lax.div(ctx, 2)

    def at_ctx(offset):
        return {"ctx": lax.rem(ctx + (offset % n_ctx), n_ctx)}

    def at_tis(offset):
        return {"tis": lax.rem(tis + (offset % n_tis), n_tis)}

    def at_rep(offset):
        return {"rep": lax.rem(rep + (offset % n_rep), n_rep)}

    other_core = {"ctx": ctx + 1 - 2 * core}

    def remote(src, dst, send, recv, device):
        return pltpu.make_async_remote_copy(
            src_ref=src,
            dst_ref=dst,
            send_sem=send,
            recv_sem=recv,
            device_id=device,
            device_id_type=MESH,
        )

    def halo(k):
        return remote(
            window.at[0], window.at[k], halo_send.at[k - 1], halo_recv.at[k - 1], at_ctx(-k)
        )

    def to_core(t):
        return remote(
            part.at[t, 1 - core], from_core.at[t], core_send.at[t], core_recv.at[t], other_core
        )

    flip = (rep + 1 - 2 * lax.rem(rep, 2), n_rep - 1 - rep)
    far = lax.rem(rep + 2, n_rep)

    def to_first(t, half):
        return remote(
            by_rep.at[t, half, pl.ds(2, 2)],
            from_first.at[t, half],
            first_send.at[t, half],
            first_recv.at[t, half],
            {"rep": flip[half]},
        )

    def to_second(t, half):
        return remote(
            by_rep.at[t, half, 1],
            from_second.at[t, half],
            second_send.at[t, half],
            second_recv.at[t, half],
            {"rep": flip[1 - half]},
        )

    def to_rep(j):
        return remote(
            last_rep.at[j - 1], from_rep.at[j - 1], rep_send.at[j - 1], rep_recv.at[j - 1], at_rep(j)
        )

    def to_z(t, j):
        return remote(
            by_z.at[t, lax.rem(z + j, n_z)],
            from_z.at[t, j - 1],
            z_send.at[t, j - 1],
            z_recv.at[t, j - 1],
            at_ctx(2 * j),
        )

    def to_ctx(k):
        return remote(
            contrib.at[k], from_ctx.at[k - 1], ctx_send.at[k - 1], ctx_recv.at[k - 1], at_ctx(k)
        )

    def to_tis(j):
        return remote(
            by_tis.at[tis], by_tis.at[tis], tis_send.at[j - 1], tis_recv.at[j - 1], at_tis(j)
        )

    def from_tis(j):
        came = lax.rem(tis + (n_tis - j), n_tis)
        return remote(
            by_tis.at[tis], by_tis.at[came], tis_send.at[j - 1], tis_recv.at[j - 1], at_tis(j)
        )

    staged = [
        pltpu.make_async_copy(src, dst, local.at[i])
        for i, (src, dst) in enumerate(
            [
                (apos_in, apos_ref),
                (dpos_in, dpos_ref),
                (don_in, don_ref),
                (acc_in.at[0], window.at[0]),
                (mask_in, mask_ref),
                (table_in, table_ref),
                (wo_in, wo_ref),
                (goal_in, goal_ref),
                (w_in, w_ref),
            ]
        )
    ]

    barrier = pltpu.get_barrier_semaphore()
    near = set(k % n_ctx for k in range(-SPAN, SPAN + 1)) | set(range(0, n_ctx, 2))
    peers = [at_ctx(k) for k in sorted(near) if k]
    peers += [at_tis(j) for j in range(1, n_tis)] + [at_rep(j) for j in range(1, n_rep)]
    for peer in peers:
        pl.semaphore_signal(barrier, inc=1, device_id=peer, device_id_type=MESH)
    for copy in staged:
        copy.start()
    for copy in staged[:-1]:
        copy.wait()
    mpad[...] = jnp.zeros_like(mpad)
    mpad[:, 0:SLOTS] = mask_ref[0].astype(F32)
    row = lax.broadcasted_iota(jnp.int32, (WIDTH, WIDTH), 0)
    col = lax.broadcasted_iota(jnp.int32, (WIDTH, WIDTH), 1)
    per_core = WIDTH // 2
    per_rep = per_core // n_rep
    deep = per_rep // n_z
    want = (
        (((row // deep) % n_z) * 2 + row // per_core) * (WIDTH // n_ctx)
        + ((row // per_rep) % n_rep) * deep
        + row % deep
    )
    perm[...] = jnp.where(col == want, 2.0, 0.0).astype(BF16)
    for t in range(tissues):
        line = wo_ref[t : t + 1, :].astype(F32)
        out_cols[t] = jnp.broadcast_to(line, (LANES, HIDDEN)).astype(BF16)
        out_rows[t] = jnp.broadcast_to(0.5 * line, (8, HIDDEN))
    eye = lax.broadcasted_iota(jnp.int32, (BLK, BLK), 0) == lax.broadcasted_iota(
        jnp.int32, (BLK, BLK), 1
    )

    def column(line):
        spread = jnp.where(eye, jnp.broadcast_to(line.astype(F32), (BLK, BLK)), 0.0)
        total = jnp.sum(spread, axis=1, keepdims=True)
        return jnp.broadcast_to(total, (BLK, LANES)).astype(jnp.int32)

    dcol = column(dpos_ref[...])
    for t in range(tissues):
        goals[t] = column(goal_ref[0, t : t + 1, :])
    pl.semaphore_wait(barrier, len(peers))

    for k in reversed(range(1, REACH)):
        halo(k).start()

    lane = lax.broadcasted_iota(jnp.int32, (BLK, BLK, LANES), 2)
    slot_in = lax.broadcasted_iota(jnp.int32, (BLK, BLK, LANES), 0)
    ones = jnp.ones((LANES, LANES), BF16)
    donors = don_ref[0].astype(F32)

    def prepare(k, carry):
        base = (ctx + k) * BLK
        dist = jnp.stack(
            [
                k * BLOCK_BP + apos_ref[0, lax.rem(base + a, n_ctx * BLK)] - dcol
                for a in range(BLK)
            ]
        )
        bins = jnp.clip(lax.shift_right_arithmetic(dist - 1, 11), 0, BINS - 1)
        lookup = jnp.where(bins == lane, 1.0, 0.0).astype(BF16).reshape(ROWS, BINS)
        table = jnp.dot(lookup, table_ref[...], preferred_element_type=F32)
        picked = jnp.where(lane == slot_in + k * BLK, mpad[...][None], 0.0)
        allowed = jnp.dot(
            picked.astype(BF16).reshape(ROWS, LANES), ones, preferred_element_type=F32
        ).reshape(BLK, BLK, LANES)
        ok = (allowed > 0.5) & (dist > 0) & (dist <= SPAN * BLOCK_BP)
        ok = jnp.where(ok, 1.0, 0.0)
        valid[pl.ds(k * BLK, BLK)] = jnp.where(ctx + k < n_ctx, ok, 0.0)
        half = 0.5 * (table.reshape(BLK, BLK, WIDTH) + donors[None])
        half_pre[pl.ds(pl.multiple_of(k * ROWS, ROWS), ROWS)] = half.reshape(ROWS, WIDTH)
        return carry

    def before(k):
        rows = pl.ds(pl.multiple_of(k * ROWS, ROWS), ROWS)
        feats = jnp.where(ctx + k < n_ctx, 0.5 * window[k].astype(F32), 0.0)
        h = half_pre[rows].reshape(BLK, BLK, WIDTH) + feats[:, None, :]
        h = h.reshape(ROWS, WIDTH)
        half_pre[rows] = h
        u = jnp.tanh(h)
        pair = 0.5 * (h + h * u).astype(BF16).astype(F32)
        half = pair.astype(BF16)
        half_pair[rows] = half
        pair_t[:, rows] = lax.dot_general(
            perm[...], half, (((1,), (1,)), ((), ())), preferred_element_type=F32
        ).astype(BF16)

    def forward(t, low, high):
        rows = slice(low * BLK, high * BLK)
        h = jnp.dot(half_pair[rows], w_ref[t], preferred_element_type=F32)
        u = jnp.tanh(h)
        p = h * u
        slope[t, rows] = (1.0 + u) * ((1.0 + h) - p)
        logit[t, low:high] = lax.dot_general(
            (h + p).astype(BF16),
            out_cols[t],
            (((1,), (1,)), ((), ())),
            preferred_element_type=F32,
        ).reshape(high - low, BLK, LANES)

    lax.fori_loop(0, REACH, prepare, 0)
    before(0)
    staged[-1].wait()

    def first_block(t, carry):
        forward(t, 0, BLK)
        return carry

    lax.fori_loop(0, tissues, first_block, 0)

    def more(k, carry):
        halo(k).wait()
        before(k)
        return carry

    lax.fori_loop(1, REACH, more, 0)

    slot_all = lax.broadcasted_iota(jnp.int32, (SLOTS, BLK, LANES), 0)
    lane_row = lax.broadcasted_iota(jnp.int32, (BLK, LANES), 1)

    def send_first(t):
        to_core(t).wait()
        for half in range(2):
            for i, q in enumerate((rep, flip[1 - half], flip[half], far)):
                rows = pl.ds(pl.multiple_of(q * per_rep, per_rep), per_rep)
                by_rep[t, half, i] = part[t, core, half, rows] + from_core[t, half, rows]
            to_first(t, half).start()

    def send_second(t):
        for half in range(2):
            to_first(t, half).wait()
            by_rep[t, half, 1] = by_rep[t, half, 1] + from_first[t, half, 1]
            to_second(t, half).start()

    def send_z(t):
        for half in range(2):
            to_second(t, half).wait()
            total = by_rep[t, half, 0] + from_first[t, half, 0] + from_second[t, half]
            for i in range(n_z):
                by_z[t, i, :, half * WIDTH : (half + 1) * WIDTH] = total[i * deep : (i + 1) * deep]
        for j in range(1, n_z):
            to_z(t, j).start()

    def send_rep(t):
        to_core(t).wait()
        for j in (2, 1, 3, 0):
            rows = pl.ds(pl.multiple_of(lax.rem(rep + j, n_rep) * per_rep, per_rep), per_rep)
            for half in range(2):
                cols = slice(half * WIDTH, (half + 1) * WIDTH)
                total = part[t, core, half, rows] + from_core[t, half, rows]
                if j:
                    last_rep[j - 1, :, cols] = total.astype(BF16)
                else:
                    last_own[:, cols] = total
            if j:
                to_rep(j).start()

    def send_last_z(t):
        total = last_own[...]
        for j in range(1, n_rep):
            to_rep(j).wait()
            total = total + from_rep[j - 1].astype(F32)
        for i in range(n_z):
            by_z[t, i] = total[i * deep : (i + 1) * deep]
        for j in range(1, n_z):
            to_z(t, j).start()

    def tissue(t, carry):
        forward(t, BLK, 3 * BLK)
        forward(t, 3 * BLK, SLOTS)

        @pl.when(t >= 3)
        def _():
            send_second(t - 3)

        raw = logit[t]
        ok = valid[...] > 0.5
        top = jnp.maximum(jnp.max(jnp.where(ok, raw, -jnp.inf), axis=0), 0.0)
        expo = jnp.where(ok, jnp.exp(raw - top[None]), 0.0)
        total = jnp.sum(expo, axis=0) + jnp.exp(-top)
        hit = goals[t][None] == slot_all
        grad_logit[...] = expo * (1.0 / total)[None] - jnp.where(hit, 1.0, 0.0)
        seen = jnp.sum(jnp.where(hit, raw, 0.0), axis=0)
        losses[t] = top + jnp.log(total) - seen

        for k in range(REACH):
            rows = slice(k * ROWS, (k + 1) * ROWS)
            gl = grad_logit[k * BLK : (k + 1) * BLK].reshape(ROWS, LANES)
            wide = jnp.concatenate([gl] * (HIDDEN // LANES), axis=1)
            grad_hid[t, rows] = ((wide * out_rows[t, 0:1]) * slope[t, rows]).astype(BF16)
        total = jnp.dot(pair_t[...], grad_hid[t], preferred_element_type=F32)
        total = total.reshape(2, per_core, HIDDEN)
        for half in range(2):
            part[t, :, half] = total[:, :, half * WIDTH : (half + 1) * WIDTH]
        to_core(t).start()

        @pl.when(t >= 1)
        def _():
            send_first(t - 1)

        return carry

    lax.fori_loop(0, tissues, tissue, 0)
    last = tissues - 1
    def after(low, high):
        rows = slice(low * ROWS, high * ROWS)
        total = None
        for t in range(tissues):
            term = lax.dot_general(
                grad_hid[t, rows],
                w_ref[t],
                (((1,), (1,)), ((), ())),
                preferred_element_type=F32,
            )
            total = term if total is None else total + term
        h = half_pre[rows]
        u = jnp.tanh(h)
        steep = 0.5 * ((1.0 + u) * ((1.0 + h) - h * u))
        grad_pre = (total * steep).reshape((high - low) * BLK, BLK, WIDTH)
        contrib[low:high] = jnp.sum(grad_pre, axis=1).reshape(high - low, BLK, WIDTH)
        for k in range(max(low, 1), high):
            to_ctx(k).start()

    after(3, REACH)
    send_second(last - 2)
    send_z(last - 3)
    send_rep(last)
    after(1, 3)
    send_second(last - 1)
    send_z(last - 2)
    after(0, 1)
    send_last_z(last)
    total = contrib[0]
    for k in range(1, REACH):
        to_ctx(k).wait()
        total = total + from_ctx[k - 1]
    by_tis[tis] = total
    for j in range(1, n_tis):
        to_tis(j).start()
    send_z(last - 1)
    wide_eye = lax.broadcasted_iota(jnp.int32, (BLK, LANES), 0) == lane_row
    for t in range(tissues):
        line = jnp.sum(jnp.where(wide_eye, losses[t], 0.0), axis=0, keepdims=True)
        loss_ref[0, t : t + 1, :] = line[:, 0:BLK]

    def finish(t, carry):
        total = by_z[t, z]
        for j in range(1, n_z):
            to_z(t, j).wait()
            total = total + from_z[t, j - 1]
        gw_ref[t] = total
        return carry

    lax.fori_loop(0, tissues, finish, 0)
    for j in range(1, n_tis):
        to_tis(j).wait_send()
        from_tis(j).wait_recv()
    total = by_tis[0]
    for j in range(1, n_tis):
        total = total + by_tis[j]
    gacc_ref[0] = total


def hand_over(*refs):
    sems = refs[6]
    copies = [
        pltpu.make_async_copy(refs[i], refs[3 + i], sems.at[i]) for i in range(3)
    ]
    for copy in copies:
        copy.start()
    for copy in copies:
        copy.wait()


def solution(mesh):
    n_ctx, n_tis, n_rep = (mesh.shape[name] for name in ("ctx", "tis", "rep"))
    n_z = n_ctx // 2

    def on_device(don, acc, dpos, apos, mask, goal, table, w, wo):
        tissues = w.shape[0]
        per_core = WIDTH // 2
        per_rep = per_core // n_rep
        deep = per_rep // n_z
        vmem = pl.BlockSpec(memory_space=pltpu.VMEM)
        hbm = pl.BlockSpec(memory_space=pltpu.HBM)
        pairs = SLOTS * BLK
        scratch = [
            pltpu.VMEM((1, BLK, WIDTH), BF16),
            pltpu.VMEM((1, BLK), jnp.int32),
            pltpu.SMEM((1, n_ctx * BLK), jnp.int32),
            pltpu.VMEM((1, BLK, SLOTS), jnp.int32),
            pltpu.VMEM((1, tissues, BLK), jnp.int32),
            pltpu.VMEM((BINS, WIDTH), BF16),
            pltpu.VMEM((tissues, WIDTH, HIDDEN), BF16),
            pltpu.VMEM((tissues, HIDDEN), BF16),
            pltpu.VMEM((REACH, BLK, WIDTH), BF16),
            pltpu.VMEM((BLK, LANES), F32),
            pltpu.VMEM((WIDTH, WIDTH), BF16),
            pltpu.VMEM((pairs, WIDTH), BF16),
            pltpu.VMEM((WIDTH, pairs), BF16),
            pltpu.VMEM((pairs, WIDTH), F32),
            pltpu.VMEM((SLOTS, BLK, LANES), F32),
            pltpu.VMEM((tissues, pairs, HIDDEN), F32),
            pltpu.VMEM((tissues, SLOTS, BLK, LANES), F32),
            pltpu.VMEM((SLOTS, BLK, LANES), F32),
            pltpu.VMEM((tissues, pairs, HIDDEN), BF16),
            pltpu.VMEM((tissues, LANES, HIDDEN), BF16),
            pltpu.VMEM((tissues, 8, HIDDEN), F32),
            pltpu.VMEM((tissues, BLK, LANES), jnp.int32),
            pltpu.VMEM((tissues, BLK, LANES), F32),
            pltpu.VMEM((tissues, 2, 2, per_core, WIDTH), F32),
            pltpu.VMEM((tissues, 2, per_core, WIDTH), F32),
            pltpu.VMEM((tissues, 2, n_rep, per_rep, WIDTH), F32),
            pltpu.VMEM((tissues, 2, 2, per_rep, WIDTH), F32),
            pltpu.VMEM((tissues, 2, per_rep, WIDTH), F32),
            pltpu.VMEM((per_rep, HIDDEN), F32),
            pltpu.VMEM((n_rep - 1, per_rep, HIDDEN), BF16),
            pltpu.VMEM((n_rep - 1, per_rep, HIDDEN), BF16),
            pltpu.VMEM((tissues, n_z, deep, HIDDEN), F32),
            pltpu.VMEM((tissues, n_z - 1, deep, HIDDEN), F32),
            pltpu.VMEM((REACH, BLK, WIDTH), F32),
            pltpu.VMEM((SPAN, BLK, WIDTH), F32),
            pltpu.VMEM((n_tis, BLK, WIDTH), F32),
            pltpu.SemaphoreType.DMA((9,)),
            pltpu.SemaphoreType.DMA((SPAN,)),
            pltpu.SemaphoreType.DMA((SPAN,)),
            pltpu.SemaphoreType.DMA((tissues,)),
            pltpu.SemaphoreType.DMA((tissues,)),
            pltpu.SemaphoreType.DMA((tissues, 2)),
            pltpu.SemaphoreType.DMA((tissues, 2)),
            pltpu.SemaphoreType.DMA((tissues, 2)),
            pltpu.SemaphoreType.DMA((tissues, 2)),
            pltpu.SemaphoreType.DMA((n_rep - 1,)),
            pltpu.SemaphoreType.DMA((n_rep - 1,)),
            pltpu.SemaphoreType.DMA((tissues, n_z - 1)),
            pltpu.SemaphoreType.DMA((tissues, n_z - 1)),
            pltpu.SemaphoreType.DMA((SPAN,)),
            pltpu.SemaphoreType.DMA((SPAN,)),
            pltpu.SemaphoreType.DMA((n_tis - 1,)),
            pltpu.SemaphoreType.DMA((n_tis - 1,)),
        ]
        results = pl.pallas_call(
            functools.partial(kernel, (n_ctx, n_tis, n_rep, tissues)),
            out_shape=(
                jax.ShapeDtypeStruct((1, tissues, BLK), F32),
                jax.ShapeDtypeStruct((tissues, deep, HIDDEN), F32),
                jax.ShapeDtypeStruct((1, BLK, WIDTH), F32),
            ),
            in_specs=[hbm] * 9,
            out_specs=(vmem, vmem, vmem),
            scratch_shapes=scratch,
            compiler_params=pltpu.CompilerParams(
                collective_id=0, has_side_effects=True, vmem_limit_bytes=60 << 20
            ),
        )(don, acc, dpos, apos, mask, jnp.swapaxes(goal, 1, 2), table, w, wo)
        loss, grad_hidden, grad_acceptor = pl.pallas_call(
            hand_over,
            out_shape=tuple(jax.ShapeDtypeStruct(r.shape, r.dtype) for r in results),
            in_specs=[vmem] * 3,
            out_specs=(hbm,) * 3,
            scratch_shapes=[pltpu.SemaphoreType.DMA((3,))],
        )(*results)
        return jnp.swapaxes(loss, 1, 2), grad_hidden, grad_acceptor

    placed = (
        P("rep", "ctx", None),
        P("rep", "ctx", None),
        P("rep", "ctx"),
        P("rep", None),
        P("rep", "ctx", None),
        P("rep", "ctx", "tis"),
        P(),
        P("tis", None, None),
        P("tis", None),
    )
    return jax.shard_map(
        on_device,
        mesh=mesh,
        in_specs=placed,
        out_specs=(P("rep", "ctx", "tis"), P("tis", ("ctx", "rep"), None), P("rep", "ctx", None)),
        check_vma=False,
    )
```

```python
import functools

import jax
import jax.numpy as jnp
from jax import lax
from jax.experimental import pallas as pl
from jax.experimental.pallas import tpu as pltpu
from jax.sharding import PartitionSpec as P

MESH = pl.DeviceIdType.MESH
F32 = jnp.float32
BF16 = jnp.bfloat16
BLOCK_BP = 65536
SPAN = 4
REACH = SPAN + 1
BIN_BP = 2048
BINS = 128
BLK = 16
ROWS = BLK * BLK
SLOTS = REACH * BLK
WIDTH = 256
HIDDEN = 512
LANES = 128


def kernel(
    sizes,
    don_in,
    acc_in,
    dpos_in,
    apos_in,
    mask_in,
    goal_in,
    table_in,
    w_in,
    wo_in,
    loss_ref,
    gw_ref,
    gacc_ref,
    don_ref,
    dpos_ref,
    apos_ref,
    mask_ref,
    goal_ref,
    table_ref,
    w_ref,
    wo_ref,
    window,
    mpad,
    perm,
    half_pair,
    pair_t,
    half_pre,
    valid,
    slope,
    logit,
    grad_logit,
    grad_hid,
    out_cols,
    out_rows,
    goals,
    losses,
    part,
    from_core,
    own_rep,
    by_rep,
    from_rep,
    by_z,
    from_z,
    contrib,
    from_ctx,
    by_tis,
    local,
    halo_send,
    halo_recv,
    core_send,
    core_recv,
    rep_send,
    rep_recv,
    z_send,
    z_recv,
    ctx_send,
    ctx_recv,
    tis_send,
    tis_recv,
):
    n_ctx, n_tis, n_rep, tissues = sizes
    n_z = n_ctx // 2
    ctx = lax.axis_index("ctx")
    tis = lax.axis_index("tis")
    rep = lax.axis_index("rep")
    core = lax.rem(ctx, 2)
    z = lax.div(ctx, 2)

    def at_ctx(offset):
        return {"ctx": lax.rem(ctx + (offset % n_ctx), n_ctx)}

    def at_tis(offset):
        return {"tis": lax.rem(tis + (offset % n_tis), n_tis)}

    def at_rep(offset):
        return {"rep": lax.rem(rep + (offset % n_rep), n_rep)}

    other_core = {"ctx": ctx + 1 - 2 * core}

    def remote(src, dst, send, recv, device):
        return pltpu.make_async_remote_copy(
            src_ref=src,
            dst_ref=dst,
            send_sem=send,
            recv_sem=recv,
            device_id=device,
            device_id_type=MESH,
        )

    def halo(k):
        return remote(
            window.at[0], window.at[k], halo_send.at[k - 1], halo_recv.at[k - 1], at_ctx(-k)
        )

    def to_core(t):
        return remote(
            part.at[t, 1 - core], from_core.at[t], core_send.at[t], core_recv.at[t], other_core
        )

    def to_rep(t, j):
        return remote(
            by_rep.at[t, j - 1],
            from_rep.at[t, j - 1],
            rep_send.at[t, j - 1],
            rep_recv.at[t, j - 1],
            at_rep(j),
        )

    def to_z(t, j):
        return remote(
            by_z.at[t, lax.rem(z + j, n_z)],
            from_z.at[t, j - 1],
            z_send.at[t, j - 1],
            z_recv.at[t, j - 1],
            at_ctx(2 * j),
        )

    def to_ctx(k):
        return remote(
            contrib.at[k], from_ctx.at[k - 1], ctx_send.at[k - 1], ctx_recv.at[k - 1], at_ctx(k)
        )

    def to_tis(j):
        return remote(
            by_tis.at[tis], by_tis.at[tis], tis_send.at[j - 1], tis_recv.at[j - 1], at_tis(j)
        )

    def from_tis(j):
        came = lax.rem(tis + (n_tis - j), n_tis)
        return remote(
            by_tis.at[tis], by_tis.at[came], tis_send.at[j - 1], tis_recv.at[j - 1], at_tis(j)
        )

    staged = [
        pltpu.make_async_copy(src, dst, local.at[i])
        for i, (src, dst) in enumerate(
            [
                (apos_in, apos_ref),
                (dpos_in, dpos_ref),
                (don_in, don_ref),
                (acc_in.at[0], window.at[0]),
                (mask_in, mask_ref),
                (table_in, table_ref),
                (wo_in, wo_ref),
                (goal_in, goal_ref),
                (w_in, w_ref),
            ]
        )
    ]

    barrier = pltpu.get_barrier_semaphore()
    near = set(k % n_ctx for k in range(-SPAN, SPAN + 1)) | set(range(0, n_ctx, 2))
    peers = [at_ctx(k) for k in sorted(near) if k]
    peers += [at_tis(j) for j in range(1, n_tis)] + [at_rep(j) for j in range(1, n_rep)]
    for peer in peers:
        pl.semaphore_signal(barrier, inc=1, device_id=peer, device_id_type=MESH)
    for copy in staged:
        copy.start()
    for copy in staged[:-1]:
        copy.wait()
    mpad[...] = jnp.zeros_like(mpad)
    mpad[:, 0:SLOTS] = mask_ref[0].astype(F32)
    row = lax.broadcasted_iota(jnp.int32, (WIDTH, WIDTH), 0)
    col = lax.broadcasted_iota(jnp.int32, (WIDTH, WIDTH), 1)
    per_core = WIDTH // 2
    per_rep = per_core // n_rep
    deep = per_rep // n_z
    want = (
        (((row // deep) % n_z) * 2 + row // per_core) * (WIDTH // n_ctx)
        + ((row // per_rep) % n_rep) * deep
        + row % deep
    )
    perm[...] = jnp.where(col == want, 2.0, 0.0).astype(BF16)
    for t in range(tissues):
        line = wo_ref[t : t + 1, :].astype(F32)
        out_cols[t] = jnp.broadcast_to(line, (LANES, HIDDEN)).astype(BF16)
        out_rows[t] = jnp.broadcast_to(0.5 * line, (8, HIDDEN))
    eye = lax.broadcasted_iota(jnp.int32, (BLK, BLK), 0) == lax.broadcasted_iota(
        jnp.int32, (BLK, BLK), 1
    )

    def column(line):
        spread = jnp.where(eye, jnp.broadcast_to(line.astype(F32), (BLK, BLK)), 0.0)
        total = jnp.sum(spread, axis=1, keepdims=True)
        return jnp.broadcast_to(total, (BLK, LANES)).astype(jnp.int32)

    dcol = column(dpos_ref[...])
    for t in range(tissues):
        goals[t] = column(goal_ref[0, t : t + 1, :])
    pl.semaphore_wait(barrier, len(peers))

    for k in reversed(range(1, REACH)):
        halo(k).start()

    lane = lax.broadcasted_iota(jnp.int32, (BLK, BLK, LANES), 2)
    slot_in = lax.broadcasted_iota(jnp.int32, (BLK, BLK, LANES), 0)
    ones = jnp.ones((LANES, LANES), BF16)
    donors = don_ref[0].astype(F32)

    def prepare(k, carry):
        base = (ctx + k) * BLK
        dist = jnp.stack(
            [
                k * BLOCK_BP + apos_ref[0, lax.rem(base + a, n_ctx * BLK)] - dcol
                for a in range(BLK)
            ]
        )
        bins = jnp.clip(lax.shift_right_arithmetic(dist - 1, 11), 0, BINS - 1)
        lookup = jnp.where(bins == lane, 1.0, 0.0).astype(BF16).reshape(ROWS, BINS)
        table = jnp.dot(lookup, table_ref[...], preferred_element_type=F32)
        picked = jnp.where(lane == slot_in + k * BLK, mpad[...][None], 0.0)
        allowed = jnp.dot(
            picked.astype(BF16).reshape(ROWS, LANES), ones, preferred_element_type=F32
        ).reshape(BLK, BLK, LANES)
        ok = (allowed > 0.5) & (dist > 0) & (dist <= SPAN * BLOCK_BP)
        ok = jnp.where(ok, 1.0, 0.0)
        valid[pl.ds(k * BLK, BLK)] = jnp.where(ctx + k < n_ctx, ok, 0.0)
        half = 0.5 * (table.reshape(BLK, BLK, WIDTH) + donors[None])
        half_pre[pl.ds(pl.multiple_of(k * ROWS, ROWS), ROWS)] = half.reshape(ROWS, WIDTH)
        return carry

    def before(k):
        rows = pl.ds(pl.multiple_of(k * ROWS, ROWS), ROWS)
        feats = jnp.where(ctx + k < n_ctx, 0.5 * window[k].astype(F32), 0.0)
        h = half_pre[rows].reshape(BLK, BLK, WIDTH) + feats[:, None, :]
        h = h.reshape(ROWS, WIDTH)
        half_pre[rows] = h
        u = jnp.tanh(h)
        pair = 0.5 * (h + h * u).astype(BF16).astype(F32)
        half = pair.astype(BF16)
        half_pair[rows] = half
        pair_t[:, rows] = lax.dot_general(
            perm[...], half, (((1,), (1,)), ((), ())), preferred_element_type=F32
        ).astype(BF16)

    def forward(t, low, high):
        rows = slice(low * BLK, high * BLK)
        h = jnp.dot(half_pair[rows], w_ref[t], preferred_element_type=F32)
        u = jnp.tanh(h)
        p = h * u
        slope[t, rows] = (1.0 + u) * ((1.0 + h) - p)
        logit[t, low:high] = lax.dot_general(
            (h + p).astype(BF16),
            out_cols[t],
            (((1,), (1,)), ((), ())),
            preferred_element_type=F32,
        ).reshape(high - low, BLK, LANES)

    lax.fori_loop(0, REACH, prepare, 0)
    before(0)
    staged[-1].wait()

    def first_block(t, carry):
        forward(t, 0, BLK)
        return carry

    lax.fori_loop(0, tissues, first_block, 0)

    def more(k, carry):
        halo(k).wait()
        before(k)
        return carry

    lax.fori_loop(1, REACH, more, 0)

    slot_all = lax.broadcasted_iota(jnp.int32, (SLOTS, BLK, LANES), 0)
    lane_row = lax.broadcasted_iota(jnp.int32, (BLK, LANES), 1)

    def send_rep(t):
        to_core(t).wait()
        for j in (2, 1, 3, 0):
            rows = pl.ds(pl.multiple_of(lax.rem(rep + j, n_rep) * per_rep, per_rep), per_rep)
            total = part[t, core, rows] + from_core[t, rows]
            if j:
                by_rep[t, j - 1] = total.astype(BF16)
                to_rep(t, j).start()
            else:
                own_rep[t] = total

    def send_z(t):
        total = own_rep[t]
        for j in range(1, n_rep):
            to_rep(t, j).wait()
            total = total + from_rep[t, j - 1].astype(F32)
        for i in range(n_z):
            by_z[t, i] = total[i * deep : (i + 1) * deep]
        for j in range(1, n_z):
            to_z(t, j).start()

    def tissue(t, carry):
        forward(t, BLK, 3 * BLK)
        forward(t, 3 * BLK, SLOTS)

        raw = logit[t]
        ok = valid[...] > 0.5
        top = jnp.maximum(jnp.max(jnp.where(ok, raw, -jnp.inf), axis=0), 0.0)
        expo = jnp.where(ok, jnp.exp(raw - top[None]), 0.0)
        total = jnp.sum(expo, axis=0) + jnp.exp(-top)
        hit = goals[t][None] == slot_all
        grad_logit[...] = expo * (1.0 / total)[None] - jnp.where(hit, 1.0, 0.0)
        seen = jnp.sum(jnp.where(hit, raw, 0.0), axis=0)
        losses[t] = top + jnp.log(total) - seen

        for k in range(REACH):
            rows = slice(k * ROWS, (k + 1) * ROWS)
            gl = grad_logit[k * BLK : (k + 1) * BLK].reshape(ROWS, LANES)
            wide = jnp.concatenate([gl] * (HIDDEN // LANES), axis=1)
            grad_hid[t, rows] = ((wide * out_rows[t, 0:1]) * slope[t, rows]).astype(BF16)
        total = jnp.dot(pair_t[...], grad_hid[t], preferred_element_type=F32)
        part[t] = total.reshape(2, per_core, HIDDEN)
        to_core(t).start()

        @pl.when(t >= 1)
        def _():
            send_rep(t - 1)

        return carry

    lax.fori_loop(0, tissues, tissue, 0)
    last = tissues - 1
    def after(low, high):
        rows = slice(low * ROWS, high * ROWS)
        total = None
        for t in range(tissues):
            term = lax.dot_general(
                grad_hid[t, rows],
                w_ref[t],
                (((1,), (1,)), ((), ())),
                preferred_element_type=F32,
            )
            total = term if total is None else total + term
        h = half_pre[rows]
        u = jnp.tanh(h)
        steep = 0.5 * ((1.0 + u) * ((1.0 + h) - h * u))
        grad_pre = (total * steep).reshape((high - low) * BLK, BLK, WIDTH)
        contrib[low:high] = jnp.sum(grad_pre, axis=1).reshape(high - low, BLK, WIDTH)
        for k in range(max(low, 1), high):
            to_ctx(k).start()

    after(3, REACH)
    send_rep(last)
    send_z(last - 3)
    after(1, 3)
    send_z(last - 2)
    after(0, 1)
    send_z(last - 1)
    send_z(last)
    total = contrib[0]
    for k in range(1, REACH):
        to_ctx(k).wait()
        total = total + from_ctx[k - 1]
    by_tis[tis] = total
    for j in range(1, n_tis):
        to_tis(j).start()
    wide_eye = lax.broadcasted_iota(jnp.int32, (BLK, LANES), 0) == lane_row
    for t in range(tissues):
        line = jnp.sum(jnp.where(wide_eye, losses[t], 0.0), axis=0, keepdims=True)
        loss_ref[0, t : t + 1, :] = line[:, 0:BLK]

    def finish(t, carry):
        total = by_z[t, z]
        for j in range(1, n_z):
            to_z(t, j).wait()
            total = total + from_z[t, j - 1]
        gw_ref[t] = total
        return carry

    lax.fori_loop(0, tissues, finish, 0)
    for j in range(1, n_tis):
        to_tis(j).wait_send()
        from_tis(j).wait_recv()
    total = by_tis[0]
    for j in range(1, n_tis):
        total = total + by_tis[j]
    gacc_ref[0] = total


def hand_over(*refs):
    sems = refs[6]
    copies = [
        pltpu.make_async_copy(refs[i], refs[3 + i], sems.at[i]) for i in range(3)
    ]
    for copy in copies:
        copy.start()
    for copy in copies:
        copy.wait()


def solution(mesh):
    n_ctx, n_tis, n_rep = (mesh.shape[name] for name in ("ctx", "tis", "rep"))
    n_z = n_ctx // 2

    def on_device(don, acc, dpos, apos, mask, goal, table, w, wo):
        tissues = w.shape[0]
        per_core = WIDTH // 2
        per_rep = per_core // n_rep
        deep = per_rep // n_z
        vmem = pl.BlockSpec(memory_space=pltpu.VMEM)
        hbm = pl.BlockSpec(memory_space=pltpu.HBM)
        pairs = SLOTS * BLK
        scratch = [
            pltpu.VMEM((1, BLK, WIDTH), BF16),
            pltpu.VMEM((1, BLK), jnp.int32),
            pltpu.SMEM((1, n_ctx * BLK), jnp.int32),
            pltpu.VMEM((1, BLK, SLOTS), jnp.int32),
            pltpu.VMEM((1, tissues, BLK), jnp.int32),
            pltpu.VMEM((BINS, WIDTH), BF16),
            pltpu.VMEM((tissues, WIDTH, HIDDEN), BF16),
            pltpu.VMEM((tissues, HIDDEN), BF16),
            pltpu.VMEM((REACH, BLK, WIDTH), BF16),
            pltpu.VMEM((BLK, LANES), F32),
            pltpu.VMEM((WIDTH, WIDTH), BF16),
            pltpu.VMEM((pairs, WIDTH), BF16),
            pltpu.VMEM((WIDTH, pairs), BF16),
            pltpu.VMEM((pairs, WIDTH), F32),
            pltpu.VMEM((SLOTS, BLK, LANES), F32),
            pltpu.VMEM((tissues, pairs, HIDDEN), F32),
            pltpu.VMEM((tissues, SLOTS, BLK, LANES), F32),
            pltpu.VMEM((SLOTS, BLK, LANES), F32),
            pltpu.VMEM((tissues, pairs, HIDDEN), BF16),
            pltpu.VMEM((tissues, LANES, HIDDEN), BF16),
            pltpu.VMEM((tissues, 8, HIDDEN), F32),
            pltpu.VMEM((tissues, BLK, LANES), jnp.int32),
            pltpu.VMEM((tissues, BLK, LANES), F32),
            pltpu.VMEM((tissues, 2, per_core, HIDDEN), F32),
            pltpu.VMEM((tissues, per_core, HIDDEN), F32),
            pltpu.VMEM((tissues, per_rep, HIDDEN), F32),
            pltpu.VMEM((tissues, n_rep - 1, per_rep, HIDDEN), BF16),
            pltpu.VMEM((tissues, n_rep - 1, per_rep, HIDDEN), BF16),
            pltpu.VMEM((tissues, n_z, deep, HIDDEN), F32),
            pltpu.VMEM((tissues, n_z - 1, deep, HIDDEN), F32),
            pltpu.VMEM((REACH, BLK, WIDTH), F32),
            pltpu.VMEM((SPAN, BLK, WIDTH), F32),
            pltpu.VMEM((n_tis, BLK, WIDTH), F32),
            pltpu.SemaphoreType.DMA((9,)),
            pltpu.SemaphoreType.DMA((SPAN,)),
            pltpu.SemaphoreType.DMA((SPAN,)),
            pltpu.SemaphoreType.DMA((tissues,)),
            pltpu.SemaphoreType.DMA((tissues,)),
            pltpu.SemaphoreType.DMA((tissues, n_rep - 1)),
            pltpu.SemaphoreType.DMA((tissues, n_rep - 1)),
            pltpu.SemaphoreType.DMA((tissues, n_z - 1)),
            pltpu.SemaphoreType.DMA((tissues, n_z - 1)),
            pltpu.SemaphoreType.DMA((SPAN,)),
            pltpu.SemaphoreType.DMA((SPAN,)),
            pltpu.SemaphoreType.DMA((n_tis - 1,)),
            pltpu.SemaphoreType.DMA((n_tis - 1,)),
        ]
        results = pl.pallas_call(
            functools.partial(kernel, (n_ctx, n_tis, n_rep, tissues)),
            out_shape=(
                jax.ShapeDtypeStruct((1, tissues, BLK), F32),
                jax.ShapeDtypeStruct((tissues, deep, HIDDEN), F32),
                jax.ShapeDtypeStruct((1, BLK, WIDTH), F32),
            ),
            in_specs=[hbm] * 9,
            out_specs=(vmem, vmem, vmem),
            scratch_shapes=scratch,
            compiler_params=pltpu.CompilerParams(
                collective_id=0, has_side_effects=True, vmem_limit_bytes=60 << 20
            ),
        )(don, acc, dpos, apos, mask, jnp.swapaxes(goal, 1, 2), table, w, wo)
        loss, grad_hidden, grad_acceptor = pl.pallas_call(
            hand_over,
            out_shape=tuple(jax.ShapeDtypeStruct(r.shape, r.dtype) for r in results),
            in_specs=[vmem] * 3,
            out_specs=(hbm,) * 3,
            scratch_shapes=[pltpu.SemaphoreType.DMA((3,))],
        )(*results)
        return jnp.swapaxes(loss, 1, 2), grad_hidden, grad_acceptor

    placed = (
        P("rep", "ctx", None),
        P("rep", "ctx", None),
        P("rep", "ctx"),
        P("rep", None),
        P("rep", "ctx", None),
        P("rep", "ctx", "tis"),
        P(),
        P("tis", None, None),
        P("tis", None),
    )
    return jax.shard_map(
        on_device,
        mesh=mesh,
        in_specs=placed,
        out_specs=(P("rep", "ctx", "tis"), P("tis", ("ctx", "rep"), None), P("rep", "ctx", None)),
        check_vma=False,
    )
```

```python
import functools

import jax
import jax.numpy as jnp
from jax import lax
from jax.experimental import pallas as pl
from jax.experimental.pallas import tpu as pltpu
from jax.sharding import PartitionSpec as P

MESH = pl.DeviceIdType.MESH
F32 = jnp.float32
BF16 = jnp.bfloat16
BLOCK_BP = 65536
SPAN = 4
REACH = SPAN + 1
BIN_BP = 2048
BINS = 128
BLK = 16
ROWS = BLK * BLK
SLOTS = REACH * BLK
WIDTH = 256
HIDDEN = 512
LANES = 128


def kernel(
    sizes,
    don_in,
    acc_in,
    dpos_in,
    apos_in,
    mask_in,
    goal_in,
    table_in,
    w_in,
    wo_in,
    loss_ref,
    gw_ref,
    gacc_ref,
    don_ref,
    dpos_ref,
    apos_ref,
    mask_ref,
    goal_ref,
    table_ref,
    w_ref,
    wo_ref,
    window,
    mpad,
    perm,
    half_pair,
    pair_t,
    half_pre,
    valid,
    slope,
    logit,
    grad_logit,
    grad_hid,
    out_cols,
    out_rows,
    goals,
    losses,
    part,
    from_core,
    own_rep,
    by_rep,
    from_rep,
    by_z,
    from_z,
    contrib,
    from_ctx,
    by_tis,
    local,
    halo_send,
    halo_recv,
    core_send,
    core_recv,
    rep_send,
    rep_recv,
    z_send,
    z_recv,
    ctx_send,
    ctx_recv,
    tis_send,
    tis_recv,
):
    n_ctx, n_tis, n_rep, tissues = sizes
    n_z = n_ctx // 2
    ctx = lax.axis_index("ctx")
    tis = lax.axis_index("tis")
    rep = lax.axis_index("rep")
    core = lax.rem(ctx, 2)
    z = lax.div(ctx, 2)

    def at_ctx(offset):
        return {"ctx": lax.rem(ctx + (offset % n_ctx), n_ctx)}

    def at_tis(offset):
        return {"tis": lax.rem(tis + (offset % n_tis), n_tis)}

    def at_rep(offset):
        return {"rep": lax.rem(rep + (offset % n_rep), n_rep)}

    other_core = {"ctx": ctx + 1 - 2 * core}

    def remote(src, dst, send, recv, device):
        return pltpu.make_async_remote_copy(
            src_ref=src,
            dst_ref=dst,
            send_sem=send,
            recv_sem=recv,
            device_id=device,
            device_id_type=MESH,
        )

    def halo(k):
        return remote(
            window.at[0], window.at[k], halo_send.at[k - 1], halo_recv.at[k - 1], at_ctx(-k)
        )

    def to_core(t):
        return remote(
            part.at[t, 1 - core], from_core.at[t], core_send.at[t], core_recv.at[t], other_core
        )

    def to_rep(t, j):
        return remote(
            by_rep.at[t, j - 1],
            from_rep.at[t, j - 1],
            rep_send.at[t, j - 1],
            rep_recv.at[t, j - 1],
            at_rep(j),
        )

    def to_z(t, j):
        return remote(
            by_z.at[t, lax.rem(z + j, n_z)],
            from_z.at[t, j - 1],
            z_send.at[t, j - 1],
            z_recv.at[t, j - 1],
            at_ctx(2 * j),
        )

    def to_ctx(k):
        return remote(
            contrib.at[k], from_ctx.at[k - 1], ctx_send.at[k - 1], ctx_recv.at[k - 1], at_ctx(k)
        )

    def to_tis(j):
        return remote(
            by_tis.at[tis], by_tis.at[tis], tis_send.at[j - 1], tis_recv.at[j - 1], at_tis(j)
        )

    def from_tis(j):
        came = lax.rem(tis + (n_tis - j), n_tis)
        return remote(
            by_tis.at[tis], by_tis.at[came], tis_send.at[j - 1], tis_recv.at[j - 1], at_tis(j)
        )

    staged = [
        pltpu.make_async_copy(src, dst, local.at[i])
        for i, (src, dst) in enumerate(
            [
                (apos_in, apos_ref),
                (dpos_in, dpos_ref),
                (don_in, don_ref),
                (acc_in.at[0], window.at[0]),
                (mask_in, mask_ref),
                (table_in, table_ref),
                (wo_in, wo_ref),
                (goal_in, goal_ref),
                (w_in, w_ref),
            ]
        )
    ]

    barrier = pltpu.get_barrier_semaphore()
    near = set(k % n_ctx for k in range(-SPAN, SPAN + 1)) | set(range(0, n_ctx, 2))
    peers = [at_ctx(k) for k in sorted(near) if k]
    peers += [at_tis(j) for j in range(1, n_tis)] + [at_rep(j) for j in range(1, n_rep)]
    for peer in peers:
        pl.semaphore_signal(barrier, inc=1, device_id=peer, device_id_type=MESH)
    for copy in staged:
        copy.start()
    for copy in staged[:-1]:
        copy.wait()

    pl.semaphore_wait(barrier, len(peers))

    for k in reversed(range(1, REACH)):
        halo(k).start()

    mpad[...] = jnp.zeros_like(mpad)
    mpad[:, 0:SLOTS] = mask_ref[0].astype(F32)
    row = lax.broadcasted_iota(jnp.int32, (WIDTH, WIDTH), 0)
    col = lax.broadcasted_iota(jnp.int32, (WIDTH, WIDTH), 1)
    per_core = WIDTH // 2
    per_rep = per_core // n_rep
    deep = per_rep // n_z
    want = (
        (((row // deep) % n_z) * 2 + row // per_core) * (WIDTH // n_ctx)
        + ((row // per_rep) % n_rep) * deep
        + row % deep
    )
    perm[...] = jnp.where(col == want, 2.0, 0.0).astype(BF16)
    for t in range(tissues):
        line = wo_ref[t : t + 1, :].astype(F32)
        out_cols[t] = jnp.broadcast_to(line, (LANES, HIDDEN)).astype(BF16)
        out_rows[t] = jnp.broadcast_to(0.5 * line, (8, HIDDEN))
    eye = lax.broadcasted_iota(jnp.int32, (BLK, BLK), 0) == lax.broadcasted_iota(
        jnp.int32, (BLK, BLK), 1
    )

    def column(line):
        spread = jnp.where(eye, jnp.broadcast_to(line.astype(F32), (BLK, BLK)), 0.0)
        total = jnp.sum(spread, axis=1, keepdims=True)
        return jnp.broadcast_to(total, (BLK, LANES)).astype(jnp.int32)

    dcol = column(dpos_ref[...])
    for t in range(tissues):
        goals[t] = column(goal_ref[0, t : t + 1, :])
    lane = lax.broadcasted_iota(jnp.int32, (BLK, BLK, LANES), 2)
    slot_in = lax.broadcasted_iota(jnp.int32, (BLK, BLK, LANES), 0)
    ones = jnp.ones((LANES, LANES), BF16)
    donors = don_ref[0].astype(F32)

    def prepare(k):
        base = (ctx + k) * BLK
        dist = jnp.stack(
            [
                k * BLOCK_BP + apos_ref[0, lax.rem(base + a, n_ctx * BLK)] - dcol
                for a in range(BLK)
            ]
        )
        bins = jnp.clip(lax.shift_right_arithmetic(dist - 1, 11), 0, BINS - 1)
        lookup = jnp.where(bins == lane, 1.0, 0.0).astype(BF16).reshape(ROWS, BINS)
        table = jnp.dot(lookup, table_ref[...], preferred_element_type=F32)
        picked = jnp.where(lane == slot_in + k * BLK, mpad[...][None], 0.0)
        allowed = jnp.dot(
            picked.astype(BF16).reshape(ROWS, LANES), ones, preferred_element_type=F32
        ).reshape(BLK, BLK, LANES)
        ok = (allowed > 0.5) & (dist > 0) & (dist <= SPAN * BLOCK_BP)
        ok = jnp.where(ok, 1.0, 0.0)
        valid[k * BLK : (k + 1) * BLK] = jnp.where(ctx + k < n_ctx, ok, 0.0)
        half = 0.5 * (table.reshape(BLK, BLK, WIDTH) + donors[None])
        half_pre[k * ROWS : (k + 1) * ROWS] = half.reshape(ROWS, WIDTH)

    def before(k):
        rows = slice(k * ROWS, (k + 1) * ROWS)
        feats = jnp.where(ctx + k < n_ctx, 0.5 * window[k].astype(F32), 0.0)
        h = half_pre[rows].reshape(BLK, BLK, WIDTH) + feats[:, None, :]
        h = h.reshape(ROWS, WIDTH)
        half_pre[rows] = h
        u = jnp.tanh(h)
        pair = 0.5 * (h + h * u).astype(BF16).astype(F32)
        half = pair.astype(BF16)
        half_pair[rows] = half
        pair_t[:, rows] = lax.dot_general(
            perm[...], half, (((1,), (1,)), ((), ())), preferred_element_type=F32
        ).astype(BF16)

    def forward(t, low, high):
        rows = slice(low * BLK, high * BLK)
        h = jnp.dot(half_pair[rows], w_ref[t], preferred_element_type=F32)
        u = jnp.tanh(h)
        p = h * u
        slope[t, rows] = (1.0 + u) * ((1.0 + h) - p)
        logit[t, low:high] = lax.dot_general(
            (h + p).astype(BF16),
            out_cols[t],
            (((1,), (1,)), ((), ())),
            preferred_element_type=F32,
        ).reshape(high - low, BLK, LANES)

    for k in range(REACH):
        prepare(k)
    before(0)
    staged[-1].wait()

    for t in range(tissues):
        forward(t, 0, BLK)
    for k in range(1, REACH):
        halo(k).wait()
        before(k)

    slot_all = lax.broadcasted_iota(jnp.int32, (SLOTS, BLK, LANES), 0)
    lane_row = lax.broadcasted_iota(jnp.int32, (BLK, LANES), 1)

    def send_rep(t):
        to_core(t).wait()
        for j in (2, 1, 3, 0):
            rows = pl.ds(pl.multiple_of(lax.rem(rep + j, n_rep) * per_rep, per_rep), per_rep)
            total = part[t, core, rows] + from_core[t, rows]
            if j:
                by_rep[t, j - 1] = total.astype(BF16)
                to_rep(t, j).start()
            else:
                own_rep[t] = total

    def send_z(t):
        total = own_rep[t]
        for j in range(1, n_rep):
            to_rep(t, j).wait()
            total = total + from_rep[t, j - 1].astype(F32)
        for i in range(n_z):
            by_z[t, i] = total[i * deep : (i + 1) * deep]
        for j in range(1, n_z):
            to_z(t, j).start()

    def tissue(t, carry):
        forward(t, BLK, 3 * BLK)
        forward(t, 3 * BLK, SLOTS)

        raw = logit[t]
        ok = valid[...] > 0.5
        top = jnp.maximum(jnp.max(jnp.where(ok, raw, -jnp.inf), axis=0), 0.0)
        expo = jnp.where(ok, jnp.exp(raw - top[None]), 0.0)
        total = jnp.sum(expo, axis=0) + jnp.exp(-top)
        hit = goals[t][None] == slot_all
        grad_logit[...] = expo * (1.0 / total)[None] - jnp.where(hit, 1.0, 0.0)
        seen = jnp.sum(jnp.where(hit, raw, 0.0), axis=0)
        losses[t] = top + jnp.log(total) - seen

        for k in range(REACH):
            rows = slice(k * ROWS, (k + 1) * ROWS)
            gl = grad_logit[k * BLK : (k + 1) * BLK].reshape(ROWS, LANES)
            wide = jnp.concatenate([gl] * (HIDDEN // LANES), axis=1)
            grad_hid[t, rows] = ((wide * out_rows[t, 0:1]) * slope[t, rows]).astype(BF16)
        total = jnp.dot(pair_t[...], grad_hid[t], preferred_element_type=F32)
        part[t] = total.reshape(2, per_core, HIDDEN)
        to_core(t).start()

        @pl.when(t >= 1)
        def _():
            send_rep(t - 1)

        return carry

    lax.fori_loop(0, tissues, tissue, 0)
    last = tissues - 1
    def after(low, high):
        rows = slice(low * ROWS, high * ROWS)
        total = None
        for t in range(tissues):
            term = lax.dot_general(
                grad_hid[t, rows],
                w_ref[t],
                (((1,), (1,)), ((), ())),
                preferred_element_type=F32,
            )
            total = term if total is None else total + term
        h = half_pre[rows]
        u = jnp.tanh(h)
        steep = 0.5 * ((1.0 + u) * ((1.0 + h) - h * u))
        grad_pre = (total * steep).reshape((high - low) * BLK, BLK, WIDTH)
        contrib[low:high] = jnp.sum(grad_pre, axis=1).reshape(high - low, BLK, WIDTH)
        for k in range(max(low, 1), high):
            to_ctx(k).start()

    after(3, REACH)
    send_rep(last)
    send_z(last - 3)
    after(1, 3)
    send_z(last - 2)
    after(0, 1)
    send_z(last - 1)
    send_z(last)
    total = contrib[0]
    for k in range(1, REACH):
        to_ctx(k).wait()
        total = total + from_ctx[k - 1]
    by_tis[tis] = total
    for j in range(1, n_tis):
        to_tis(j).start()
    wide_eye = lax.broadcasted_iota(jnp.int32, (BLK, LANES), 0) == lane_row
    for t in range(tissues):
        line = jnp.sum(jnp.where(wide_eye, losses[t], 0.0), axis=0, keepdims=True)
        loss_ref[0, t : t + 1, :] = line[:, 0:BLK]

    def finish(t, carry):
        total = by_z[t, z]
        for j in range(1, n_z):
            to_z(t, j).wait()
            total = total + from_z[t, j - 1]
        gw_ref[t] = total
        return carry

    lax.fori_loop(0, tissues, finish, 0)
    for j in range(1, n_tis):
        to_tis(j).wait_send()
        from_tis(j).wait_recv()
    total = by_tis[0]
    for j in range(1, n_tis):
        total = total + by_tis[j]
    gacc_ref[0] = total


def hand_over(*refs):
    sems = refs[6]
    copies = [
        pltpu.make_async_copy(refs[i], refs[3 + i], sems.at[i]) for i in range(3)
    ]
    for copy in copies:
        copy.start()
    for copy in copies:
        copy.wait()


def solution(mesh):
    n_ctx, n_tis, n_rep = (mesh.shape[name] for name in ("ctx", "tis", "rep"))
    n_z = n_ctx // 2

    def on_device(don, acc, dpos, apos, mask, goal, table, w, wo):
        tissues = w.shape[0]
        per_core = WIDTH // 2
        per_rep = per_core // n_rep
        deep = per_rep // n_z
        vmem = pl.BlockSpec(memory_space=pltpu.VMEM)
        hbm = pl.BlockSpec(memory_space=pltpu.HBM)
        pairs = SLOTS * BLK
        scratch = [
            pltpu.VMEM((1, BLK, WIDTH), BF16),
            pltpu.VMEM((1, BLK), jnp.int32),
            pltpu.SMEM((1, n_ctx * BLK), jnp.int32),
            pltpu.VMEM((1, BLK, SLOTS), jnp.int32),
            pltpu.VMEM((1, tissues, BLK), jnp.int32),
            pltpu.VMEM((BINS, WIDTH), BF16),
            pltpu.VMEM((tissues, WIDTH, HIDDEN), BF16),
            pltpu.VMEM((tissues, HIDDEN), BF16),
            pltpu.VMEM((REACH, BLK, WIDTH), BF16),
            pltpu.VMEM((BLK, LANES), F32),
            pltpu.VMEM((WIDTH, WIDTH), BF16),
            pltpu.VMEM((pairs, WIDTH), BF16),
            pltpu.VMEM((WIDTH, pairs), BF16),
            pltpu.VMEM((pairs, WIDTH), F32),
            pltpu.VMEM((SLOTS, BLK, LANES), F32),
            pltpu.VMEM((tissues, pairs, HIDDEN), F32),
            pltpu.VMEM((tissues, SLOTS, BLK, LANES), F32),
            pltpu.VMEM((SLOTS, BLK, LANES), F32),
            pltpu.VMEM((tissues, pairs, HIDDEN), BF16),
            pltpu.VMEM((tissues, LANES, HIDDEN), BF16),
            pltpu.VMEM((tissues, 8, HIDDEN), F32),
            pltpu.VMEM((tissues, BLK, LANES), jnp.int32),
            pltpu.VMEM((tissues, BLK, LANES), F32),
            pltpu.VMEM((tissues, 2, per_core, HIDDEN), F32),
            pltpu.VMEM((tissues, per_core, HIDDEN), F32),
            pltpu.VMEM((tissues, per_rep, HIDDEN), F32),
            pltpu.VMEM((tissues, n_rep - 1, per_rep, HIDDEN), BF16),
            pltpu.VMEM((tissues, n_rep - 1, per_rep, HIDDEN), BF16),
            pltpu.VMEM((tissues, n_z, deep, HIDDEN), F32),
            pltpu.VMEM((tissues, n_z - 1, deep, HIDDEN), F32),
            pltpu.VMEM((REACH, BLK, WIDTH), F32),
            pltpu.VMEM((SPAN, BLK, WIDTH), F32),
            pltpu.VMEM((n_tis, BLK, WIDTH), F32),
            pltpu.SemaphoreType.DMA((9,)),
            pltpu.SemaphoreType.DMA((SPAN,)),
            pltpu.SemaphoreType.DMA((SPAN,)),
            pltpu.SemaphoreType.DMA((tissues,)),
            pltpu.SemaphoreType.DMA((tissues,)),
            pltpu.SemaphoreType.DMA((tissues, n_rep - 1)),
            pltpu.SemaphoreType.DMA((tissues, n_rep - 1)),
            pltpu.SemaphoreType.DMA((tissues, n_z - 1)),
            pltpu.SemaphoreType.DMA((tissues, n_z - 1)),
            pltpu.SemaphoreType.DMA((SPAN,)),
            pltpu.SemaphoreType.DMA((SPAN,)),
            pltpu.SemaphoreType.DMA((n_tis - 1,)),
            pltpu.SemaphoreType.DMA((n_tis - 1,)),
        ]
        results = pl.pallas_call(
            functools.partial(kernel, (n_ctx, n_tis, n_rep, tissues)),
            out_shape=(
                jax.ShapeDtypeStruct((1, tissues, BLK), F32),
                jax.ShapeDtypeStruct((tissues, deep, HIDDEN), F32),
                jax.ShapeDtypeStruct((1, BLK, WIDTH), F32),
            ),
            in_specs=[hbm] * 9,
            out_specs=(vmem, vmem, vmem),
            scratch_shapes=scratch,
            compiler_params=pltpu.CompilerParams(
                collective_id=0, has_side_effects=True, vmem_limit_bytes=60 << 20
            ),
        )(don, acc, dpos, apos, mask, jnp.swapaxes(goal, 1, 2), table, w, wo)
        loss, grad_hidden, grad_acceptor = pl.pallas_call(
            hand_over,
            out_shape=tuple(jax.ShapeDtypeStruct(r.shape, r.dtype) for r in results),
            in_specs=[vmem] * 3,
            out_specs=(hbm,) * 3,
            scratch_shapes=[pltpu.SemaphoreType.DMA((3,))],
        )(*results)
        return jnp.swapaxes(loss, 1, 2), grad_hidden, grad_acceptor

    placed = (
        P("rep", "ctx", None),
        P("rep", "ctx", None),
        P("rep", "ctx"),
        P("rep", None),
        P("rep", "ctx", None),
        P("rep", "ctx", "tis"),
        P(),
        P("tis", None, None),
        P("tis", None),
    )
    return jax.shard_map(
        on_device,
        mesh=mesh,
        in_specs=placed,
        out_specs=(P("rep", "ctx", "tis"), P("tis", ("ctx", "rep"), None), P("rep", "ctx", None)),
        check_vma=False,
    )
```
